256 devices in a mesh: cell: 64 (over z, x, core), snap: 4 (over y).
Axes of the slice: x: 4, y: 4, z: 8, core: 2. Of those that a mesh axis runs over, the one named last changes fastest.
Arguments:
- snapshots: bfloat16 [262144, 1024], P('cell', 'snap'), may hold values from -160 to 160
Outputs:
- modes: float32 [262144, 256], P(('cell', 'snap'))
- coeffs: float32 [256, 1024], P(None, 'snap')
The draws below stay inside these ranges and needn't reach their ends.
All inputs are finite; a program needn't handle non-finite values.
Results may differ from the reference program's by a relative error of at most 0.0029.
Values may be sent and summed in bfloat16 or wider, within the bound.
No kernel may reach another device: no remote copies, remote signals or barrier semaphores. Data moves between devices by JAX's collectives and lax.ppermute only.
A program may use at most 64 MiB of HBM per device.

```python
import math
import jax
import jax.numpy as jnp
from jax import lax

SNAP_DEV = 256
LEVELS = 2
CELLS = 262144
SNAPS = 1024
N_SNAP = 4


def draw_snapshots(key, part):
    key_rows, key_cols, key_base = jax.random.split(jax.random.fold_in(key, 17), 3)
    ramp = 1.0 + 2.0 * jnp.arange(CELLS, dtype=jnp.float32)[:, None] / CELLS
    row_scale = jnp.exp(jax.random.uniform(key_rows, (CELLS, 1), jnp.float32, 0.0, math.log(10.0))) * ramp
    col_scale = jnp.exp(jax.random.uniform(key_cols, (1, SNAPS), jnp.float32, 0.0, math.log(3.0)))
    base = jnp.clip(jax.random.normal(key_base, (CELLS, SNAPS), jnp.float32), -1.7, 1.7)
    values = row_scale * col_scale * base / 3.0
    return values.astype(jnp.bfloat16)


def setup_inputs(seed: int = 0) -> dict:
    keys = jax.random.split(jax.random.key(seed), 2)
    return {
        "snapshots": draw_snapshots(jax.random.fold_in(keys[1], 71), 0),
    }


def merge_pair(stacked, need_panel):
    hi = lax.Precision.HIGHEST
    half_cols = stacked.shape[1] // 2
    panel_gram = jnp.dot(stacked.T.astype(jnp.float32), stacked.astype(jnp.float32), preferred_element_type=jnp.float32)
    projection = panel_gram[:, :half_cols] + panel_gram[:, half_cols:]
    powered = jnp.dot(stacked.astype(jnp.float32), projection.astype(jnp.float32), precision=hi, preferred_element_type=jnp.float32)
    gram_power = jnp.dot(powered.T, powered, precision=hi)
    lower_factor = jnp.linalg.cholesky(gram_power)
    basis_cols = jax.scipy.linalg.solve_triangular(lower_factor, powered.T, lower=True).T
    next_panel = None
    if need_panel:
        weights = jnp.dot(stacked.T.astype(jnp.float32), basis_cols.astype(jnp.float32), precision=hi, preferred_element_type=jnp.float32)
        energy = jnp.dot(weights.T, weights, precision=hi)
        upper_factor = jnp.linalg.cholesky(energy).T
        next_panel = jnp.dot(basis_cols, upper_factor, precision=hi).astype(jnp.bfloat16)
    return (basis_cols, next_panel)

def reference(snapshots):
    panels = [snapshots[:, group_id * SNAP_DEV:(group_id + 1) * SNAP_DEV] for group_id in range(N_SNAP)]
    basis_cols = None
    for tree_level in range(LEVELS):
        need_panel = tree_level + 1 < LEVELS
        next_panels = []
        for group_id in range(len(panels) // 2):
            stacked = jnp.concatenate([panels[2 * group_id], panels[2 * group_id + 1]], axis=1)
            basis_cols, next_panel = merge_pair(stacked, need_panel)
            next_panels.append(next_panel)
        panels = next_panels
    root_cells = jnp.sqrt(jnp.float32(CELLS))
    modes = basis_cols * root_cells
    coeffs = jnp.dot(basis_cols.T.astype(jnp.float32), snapshots.astype(jnp.float32), precision=lax.Precision.HIGHEST, preferred_element_type=jnp.float32) / root_cells
    return (modes, coeffs)
```

```python
import jax
import jax.numpy as jnp
from jax import lax
from jax.sharding import Mesh, PartitionSpec as P

HI = lax.Precision.HIGHEST
BLOCKS = [(0, 0), (0, 1), (1, 1), (2, 2), (2, 3), (3, 3), (0, 2), (0, 3), (1, 2), (1, 3)]


def hdot(a, b):
    return jnp.dot(a, b, precision=HI, preferred_element_type=jnp.float32)


def inverse_lower(lower):
    return jax.scipy.linalg.solve_triangular(lower, jnp.eye(lower.shape[0], dtype=lower.dtype), lower=True)


def reduce_gram(blocks):
    rows, width = blocks.shape
    half = rows // 2
    ring = lax.axis_size("x") * lax.axis_size("y")
    planes = lax.axis_size("z")
    part = lax.all_to_all(blocks.reshape(2, half, width), "core", 0, 0).sum(0)
    piece = half // ring
    part = lax.all_to_all(part.reshape(ring, piece, width), ("x", "y"), 0, 0).sum(0)
    part = lax.all_to_all(jnp.broadcast_to(part, (planes, piece, width)), "z", 0, 0).sum(0)
    part = lax.all_to_all(jnp.broadcast_to(part, (ring, piece, width)), ("x", "y"), 0, 0).reshape(half, width)
    part = lax.all_to_all(jnp.broadcast_to(part, (2, half, width)), "core", 0, 0)
    return part.reshape(rows, width)


def on_device(snapshots):
    cell_rows, width = snapshots.shape
    n_snap = lax.axis_size("y")
    position = lax.axis_index("y")
    share = cell_rows // n_snap
    cells = cell_rows * lax.axis_size("z") * lax.axis_size("x") * lax.axis_size("core")
    root_cells = jnp.sqrt(jnp.float32(cells))
    own = lax.all_to_all(snapshots.reshape(n_snap, share, width), "y", 0, 0)
    rows = own.transpose(1, 0, 2).reshape(share, n_snap * width)
    full = jnp.dot(rows.T, rows, preferred_element_type=jnp.float32)
    tile = lambda i, j: full[i * width : (i + 1) * width, j * width : (j + 1) * width]
    total = reduce_gram(jnp.concatenate([tile(i, j) for i, j in BLOCKS], axis=0))
    gram = {}
    for k, (i, j) in enumerate(BLOCKS):
        gram[i, j] = total[k * width : (k + 1) * width]
        if i != j:
            gram[j, i] = gram[i, j].T
    square = lambda ii, jj: jnp.concatenate([jnp.concatenate([gram[i, j] for j in jj], 1) for i in ii], 0)

    def merge(stacked_gram):
        projection = stacked_gram[:, :width] + stacked_gram[:, width:]
        image = hdot(stacked_gram, projection)
        lower = jnp.linalg.cholesky(hdot(projection.T, image))
        inverse = inverse_lower(lower)
        return hdot(projection, inverse.T), hdot(image, inverse.T)

    maps, energies = [], []
    for pair in ((0, 1), (2, 3)):
        to_basis, weights = merge(square(pair, pair))
        energy = hdot(weights.T, weights)
        maps.append(hdot(to_basis, jnp.linalg.cholesky(energy).T))
        energies.append(energy)
    cross = hdot(maps[0].T, hdot(square((0, 1), (2, 3)), maps[1]))
    top = jnp.concatenate([energies[0], cross], 1)
    bottom = jnp.concatenate([cross.T, energies[1]], 1)
    to_basis, _ = merge(jnp.concatenate([top, bottom], 0))
    panels = [
        hdot(rows[:, 2 * k * width : 2 * (k + 1) * width].astype(jnp.float32), maps[k]).astype(jnp.bfloat16)
        for k in range(2)
    ]
    modes = hdot(jnp.concatenate(panels, 1).astype(jnp.float32), to_basis * root_cells)
    all_cols = jnp.stack([square((0, 1, 2, 3), (j,)) for j in range(4)])
    own_cols = lax.dynamic_index_in_dim(all_cols, position, 0, keepdims=False)
    seen = jnp.concatenate(
        [hdot(maps[k].T, own_cols[2 * k * width : 2 * (k + 1) * width]) for k in range(2)], 0
    )
    coeffs = hdot(to_basis.T, seen) / root_cells
    return modes, coeffs


def solution(mesh):
    n_cell, n_snap = mesh.devices.shape
    cores, across = 2, 4
    fine = Mesh(
        mesh.devices.reshape(n_cell // (cores * across), across, cores, n_snap), ("z", "x", "core", "y")
    )
    cell = ("z", "x", "core")
    return jax.shard_map(
        on_device,
        mesh=fine,
        in_specs=(P(cell, "y"),),
        out_specs=(P(cell + ("y",), None), P(None, "y")),
        check_vma=False,
    )
```

```python
import functools
import jax
import jax.numpy as jnp
from jax import lax
from jax.experimental import pallas as pl
from jax.experimental.pallas import tpu as pltpu
from jax.sharding import Mesh, PartitionSpec as P

HI = lax.Precision.HIGHEST
BLOCKS = [(0, 0), (0, 1), (1, 1), (2, 2), (2, 3), (3, 3), (0, 2), (0, 3), (1, 2), (1, 3)]
NN = (((1,), (0,)), ((), ()))
NT = (((1,), (1,)), ((), ()))
EDGE = 128


def exact(a, b, dims=NN):
    return lax.dot_general(a, b, dims, precision=HI, preferred_element_type=jnp.float32)


def split(a):
    high = a.astype(jnp.bfloat16)
    return high, (a - high.astype(jnp.float32)).astype(jnp.bfloat16)


def single(a, b, dims=NN):
    return lax.dot_general(a, b, dims, preferred_element_type=jnp.float32)


def eliminate(blocks, ahead, need_inverse):
    tiles = EDGE // 8
    sub = lax.broadcasted_iota(jnp.int32, (8, EDGE), 0)
    lane = lax.broadcasted_iota(jnp.int32, (8, EDGE), 1)
    spread = lambda value: jnp.broadcast_to(value, (8, EDGE))
    states = []
    for block in blocks:
        left = [block[8 * u : 8 * u + 8] for u in range(tiles)]
        right = [jnp.where(lane == sub + 8 * u, 1.0, 0.0) for u in range(tiles)] if need_inverse else None
        cols = {c: [spread(left[u][:, c : c + 1]) for u in range(tiles)] for c in range(ahead)}
        states.append((left, right, cols, [spread(jnp.ones((1, 1), jnp.float32))] * tiles))
    for j in range(EDGE):
        t, s = divmod(j, 8)
        for left, right, cols, pivots in states:
            col = cols.pop(j)
            pivot = spread(col[t][s : s + 1, :])
            inverse = 1.0 / pivot
            pivots[t] = jnp.where(sub == s, pivot, pivots[t])
            factor = [None] * tiles
            for u in range(t, tiles):
                factor[u] = (jnp.where(sub > s, col[u], 0.0) if u == t else col[u]) * inverse
            for c in range(j + 1, min(j + ahead, EDGE)):
                entry = spread(cols[c][t][s : s + 1, :])
                cols[c] = [None if u < t else cols[c][u] - factor[u] * entry for u in range(tiles)]
            row = spread(left[t][s : s + 1, :])
            for u in range(t, tiles):
                left[u] = left[u] - factor[u] * row
            if need_inverse:
                row = spread(right[t][s : s + 1, :])
                for u in range(t, tiles):
                    right[u] = right[u] - factor[u] * row
            c = j + ahead
            if c < EDGE:
                cols[c] = [None if u < t else spread(left[u][:, c : c + 1]) for u in range(tiles)]
    results = []
    for left, right, _, pivots in states:
        scale = [lax.rsqrt(p) for p in pivots]
        upper = jnp.concatenate([jnp.where(lane >= sub + 8 * u, left[u] * scale[u], 0.0) for u in range(tiles)], 0)
        inverse = jnp.concatenate([right[u] * scale[u] for u in range(tiles)], 0) if need_inverse else None
        results.append((upper, inverse))
    return results


def tree_kernel(place_ref, mine_ref, other_ref, own_ref, modes_ref, coeffs_ref, pt, tt, wt, lp, mt, en, li, x, g2, h, mhi, mlo, *, scale):
    f32 = jnp.float32
    width = 256
    n = EDGE
    core = place_ref[1]

    def block(i, j):
        half, slot = divmod(BLOCKS.index((i, j)), len(BLOCKS) // 2)
        rows = slice(slot * width, (slot + 1) * width)
        return jnp.where(core == half, mine_ref[rows], other_ref[rows]) * scale

    top, bottom = slice(0, n), slice(n, 2 * n)
    first, second = slice(0, width), slice(width, 2 * width)

    def factor(mats, ahead):
        heads = eliminate([m[top, top] for m in mats], ahead, True)
        tails, lowers = [], []
        for m, (_, inv) in zip(mats, heads):
            low = exact(m[bottom, top], inv, NT)
            lowers.append(low)
            tails.append(m[bottom, bottom] - exact(low, low, NT))
        ends = eliminate(tails, ahead, True)
        for k, ((_, inv), (_, inv2), low) in enumerate(zip(heads, ends, lowers)):
            li[k, top, top] = inv
            li[k, top, bottom] = jnp.zeros((n, n), f32)
            li[k, bottom, bottom] = inv2
            li[k, bottom, top] = -exact(inv2, exact(low, inv))

    def lower_factor(mats, ahead):
        heads = eliminate([m[top, top] for m in mats], ahead, True)
        tails = []
        for k, (m, (up, inv)) in enumerate(zip(mats, heads)):
            low = exact(m[bottom, top], inv, NT)
            li[k, top, top] = up.T
            li[k, top, bottom] = jnp.zeros((n, n), f32)
            li[k, bottom, top] = low
            tails.append(m[bottom, bottom] - exact(low, low, NT))
        for k, (up, _) in enumerate(eliminate(tails, ahead, False)):
            li[k, bottom, bottom] = up.T

    for k in range(2):
        a, b = 2 * k, 2 * k + 1
        corner = block(a, b)
        g2[first, first] = block(a, a)
        g2[first, second] = corner
        g2[second, first] = corner.T
        g2[second, second] = block(b, b)
        pt[k] = g2[first, :] + g2[second, :]
        tt[k] = exact(pt[k], g2[...])
        en[k] = exact(pt[k], tt[k], NT)
    for i in range(2):
        for j in range(2):
            x[i * width : (i + 1) * width, j * width : (j + 1) * width] = block(i, 2 + j)
    factor([en.at[0], en.at[1]], 4)
    for k in range(2):
        wt[k] = exact(li[k], tt[k])
        lp[k] = exact(li[k], pt[k])
        en[k] = exact(wt[k], wt[k], NT)
    lower_factor([en.at[0], en.at[1]], 4)
    for k in range(2):
        mt[k] = exact(li[k], lp[k])
        mhi[k], mlo[k] = split(mt[k])
        inside = exact(li[k], wt[k])
        rows = slice(k * width, (k + 1) * width)
        h[2 * k, rows] = inside[:, first]
        h[2 * k + 1, rows] = inside[:, second]
    ahead0 = exact(mt[0], x[...])
    h[2, first] = ahead0[:, first]
    h[3, first] = ahead0[:, second]
    ahead1 = exact(mt[1], x[...], NT)
    h[0, second] = ahead1[:, first]
    h[1, second] = ahead1[:, second]
    cross = exact(ahead0, mt[1], NT)
    g2[first, first] = en[0]
    g2[first, second] = cross
    g2[second, first] = cross.T
    g2[second, second] = en[1]
    pt[0] = g2[first, :] + g2[second, :]
    tt[0] = exact(pt[0], g2[...])
    en[0] = exact(pt[0], tt[0], NT)
    factor([en.at[0]], 6)
    pt[1] = exact(li[0], pt[0])
    coeffs_ref[...] = exact(pt[1], h[place_ref[0]])
    khi, klo = split(pt[1])
    share = own_ref.shape[1]
    step = min(share, 256)
    for r in range(share // step):
        rows = slice(r * step, (r + 1) * step)
        total = None
        for k in range(2):
            panel = None
            for b in range(2):
                cols = slice(b * width, (b + 1) * width)
                part = own_ref[2 * k + b, rows]
                term = single(part, mhi[k, :, cols], NT) + single(part, mlo[k, :, cols], NT)
                panel = term if panel is None else panel + term
            panel = panel.astype(jnp.bfloat16)
            cols = slice(k * width, (k + 1) * width)
            term = single(panel, khi[:, cols], NT) + single(panel, klo[:, cols], NT)
            total = term if total is None else total + term
        modes_ref[rows] = total


def tree(place, mine, other, own, scale):
    f32 = jnp.float32
    vm = pl.BlockSpec(memory_space=pltpu.VMEM)
    return pl.pallas_call(
        functools.partial(tree_kernel, scale=scale),
        out_shape=(jax.ShapeDtypeStruct((own.shape[1], 256), f32), jax.ShapeDtypeStruct((256, 256), f32)),
        in_specs=[pl.BlockSpec(memory_space=pltpu.SMEM), vm, vm, vm],
        out_specs=(vm, vm),
        scratch_shapes=[
            pltpu.VMEM((2, 256, 512), f32),
            pltpu.VMEM((2, 256, 512), f32),
            pltpu.VMEM((2, 256, 512), f32),
            pltpu.VMEM((2, 256, 512), f32),
            pltpu.VMEM((2, 256, 512), f32),
            pltpu.VMEM((2, 256, 256), f32),
            pltpu.VMEM((2, 256, 256), f32),
            pltpu.VMEM((512, 512), f32),
            pltpu.VMEM((512, 512), f32),
            pltpu.VMEM((4, 512, 256), f32),
            pltpu.VMEM((2, 256, 512), jnp.bfloat16),
            pltpu.VMEM((2, 256, 512), jnp.bfloat16),
        ],
        compiler_params=pltpu.CompilerParams(vmem_limit_bytes=48 << 20),
        name="tree",
    )(place, mine, other, own)


def gram_kernel(place_ref, own_ref, keep_ref, send_ref):
    width = own_ref.shape[2]
    half = len(BLOCKS) // 2
    for k, (i, j) in enumerate(BLOCKS):
        value = lax.dot_general(own_ref[i], own_ref[j], (((0,), (0,)), ((), ())), preferred_element_type=jnp.float32)
        rows = slice(k % half * width, (k % half + 1) * width)

        @pl.when(place_ref[1] == k // half)
        def _():
            keep_ref[rows] = value

        @pl.when(place_ref[1] != k // half)
        def _():
            send_ref[rows] = value


def gram_halves(place, own):
    width = own.shape[2]
    vm = pl.BlockSpec(memory_space=pltpu.VMEM)
    half = jax.ShapeDtypeStruct((len(BLOCKS) // 2 * width, width), jnp.float32)
    return pl.pallas_call(
        gram_kernel,
        out_shape=(half, half),
        in_specs=[pl.BlockSpec(memory_space=pltpu.SMEM), vm],
        out_specs=(vm, vm),
        compiler_params=pltpu.CompilerParams(vmem_limit_bytes=24 << 20),
        name="gram",
    )(place, own)


def swap_cores(value):
    return lax.ppermute(value, "core", [(0, 1), (1, 0)])


def sum_everywhere(part):
    rows, width = part.shape
    ring = lax.axis_size("x") * lax.axis_size("y")
    planes = lax.axis_size("z")
    piece = rows // ring
    part = lax.all_to_all(part.reshape(ring, piece, width), ("x", "y"), 0, 0).sum(0)
    part = lax.all_to_all(jnp.broadcast_to(part, (planes, piece, width)), "z", 0, 0).sum(0)
    return lax.all_to_all(jnp.broadcast_to(part, (ring, piece, width)), ("x", "y"), 0, 0).reshape(rows, width)


def on_device(snapshots):
    cell_rows, width = snapshots.shape
    n_snap = lax.axis_size("y")
    share = cell_rows // n_snap
    cells = cell_rows * lax.axis_size("z") * lax.axis_size("x") * lax.axis_size("core")
    place = jnp.stack([lax.axis_index("y"), lax.axis_index("core")]).astype(jnp.int32)
    own = lax.all_to_all(snapshots.reshape(n_snap, share, width), "y", 0, 0)
    keep, send = gram_halves(place, own)
    mine = sum_everywhere(keep + swap_cores(send))
    return tree(place, mine, swap_cores(mine), own, 1.0 / cells)


def solution(mesh):
    n_cell, n_snap = mesh.devices.shape
    cores, across = 2, 4
    fine = Mesh(
        mesh.devices.reshape(n_cell // (cores * across), across, cores, n_snap), ("z", "x", "core", "y")
    )
    cell = ("z", "x", "core")
    return jax.shard_map(
        on_device,
        mesh=fine,
        in_specs=(P(cell, "y"),),
        out_specs=(P(cell + ("y",), None), P(None, "y")),
        check_vma=False,
    )
```

```python
import functools
import jax
import jax.numpy as jnp
from jax import lax
from jax.experimental import pallas as pl
from jax.experimental.pallas import tpu as pltpu
from jax.sharding import Mesh, PartitionSpec as P

HI = lax.Precision.HIGHEST
HALVES = (((0, 0), (0, 1), (1, 1), (0, 2), (0, 3)), ((2, 2), (2, 3), (3, 3), (1, 2), (1, 3)))
OWN = 3
NN = (((1,), (0,)), ((), ()))
NT = (((1,), (1,)), ((), ()))
EDGE = 128


def exact(a, b, dims=NN):
    return lax.dot_general(a, b, dims, precision=HI, preferred_element_type=jnp.float32)


def split(a):
    high = a.astype(jnp.bfloat16)
    return high, (a - high.astype(jnp.float32)).astype(jnp.bfloat16)


def single(a, b, dims=NN):
    return lax.dot_general(a, b, dims, preferred_element_type=jnp.float32)


def eliminate(blocks, ahead, need_inverse):
    tiles = EDGE // 8
    sub = lax.broadcasted_iota(jnp.int32, (8, EDGE), 0)
    lane = lax.broadcasted_iota(jnp.int32, (8, EDGE), 1)
    spread = lambda value: jnp.broadcast_to(value, (8, EDGE))
    states = []
    for block in blocks:
        left = [block[8 * u : 8 * u + 8] for u in range(tiles)]
        right = [jnp.where(lane == sub + 8 * u, 1.0, 0.0) for u in range(tiles)] if need_inverse else None
        cols = {c: [spread(left[u][:, c : c + 1]) for u in range(tiles)] for c in range(ahead)}
        states.append((left, right, cols, [spread(jnp.ones((1, 1), jnp.float32))] * tiles))
    for j in range(EDGE):
        t, s = divmod(j, 8)
        for left, right, cols, pivots in states:
            col = cols.pop(j)
            pivot = spread(col[t][s : s + 1, :])
            inverse = 1.0 / pivot
            pivots[t] = jnp.where(sub == s, pivot, pivots[t])
            factor = [None] * tiles
            for u in range(t, tiles):
                factor[u] = (jnp.where(sub > s, col[u], 0.0) if u == t else col[u]) * inverse
            for c in range(j + 1, min(j + ahead, EDGE)):
                entry = spread(cols[c][t][s : s + 1, :])
                cols[c] = [None if u < t else cols[c][u] - factor[u] * entry for u in range(tiles)]
            row = spread(left[t][s : s + 1, :])
            for u in range(t, tiles):
                left[u] = left[u] - factor[u] * row
            if need_inverse:
                row = spread(right[t][s : s + 1, :])
                for u in range(t, tiles):
                    right[u] = right[u] - factor[u] * row
            c = j + ahead
            if c < EDGE:
                cols[c] = [None if u < t else spread(left[u][:, c : c + 1]) for u in range(tiles)]
    results = []
    for left, right, _, pivots in states:
        scale = [lax.rsqrt(p) for p in pivots]
        upper = jnp.concatenate([jnp.where(lane >= sub + 8 * u, left[u] * scale[u], 0.0) for u in range(tiles)], 0)
        inverse = jnp.concatenate([right[u] * scale[u] for u in range(tiles)], 0) if need_inverse else None
        results.append((upper, inverse))
    return results


def set_factor(gram, inverse, ahead=6):
    n = EDGE
    top, bottom = slice(0, n), slice(n, 2 * n)
    ((_, head),) = eliminate([gram[top, top]], ahead, True)
    low = exact(gram[bottom, top], head, NT)
    ((_, tail),) = eliminate([gram[bottom, bottom] - exact(low, low, NT)], ahead, True)
    inverse[top, top] = head
    inverse[top, bottom] = jnp.zeros((n, n), jnp.float32)
    inverse[bottom, bottom] = tail
    inverse[bottom, top] = -exact(tail, exact(low, head))


def set_lower(gram, lower, ahead=6):
    n = EDGE
    top, bottom = slice(0, n), slice(n, 2 * n)
    ((upper, head),) = eliminate([gram[top, top]], ahead, True)
    low = exact(gram[bottom, top], head, NT)
    ((tail, _),) = eliminate([gram[bottom, bottom] - exact(low, low, NT)], ahead, False)
    lower[top, top] = upper.T
    lower[top, bottom] = jnp.zeros((n, n), jnp.float32)
    lower[bottom, top] = low
    lower[bottom, bottom] = tail.T


def pair_kernel(pair_ref, mt_ref, energy_ref, inside_ref, g, pt, tt, wt, small, li, *, scale):
    width = pair_ref.shape[1]
    first, second = slice(0, width), slice(width, 2 * width)
    corner = pair_ref[second] * scale
    g[first, first] = pair_ref[first] * scale
    g[first, second] = corner
    g[second, first] = corner.T
    g[second, second] = pair_ref[2 * width : 3 * width] * scale
    pt[...] = g[first, :] + g[second, :]
    tt[...] = exact(pt[...], g[...])
    small[...] = exact(pt[...], tt[...], NT)
    set_factor(small, li)
    wt[...] = exact(li[...], tt[...])
    pt[...] = exact(li[...], pt[...])
    energy_ref[...] = exact(wt[...], wt[...], NT)
    set_lower(energy_ref, li)
    mt_ref[...] = exact(li[...], pt[...])
    inside_ref[...] = exact(li[...], wt[...])


def vmem():
    return pl.BlockSpec(memory_space=pltpu.VMEM)


def smem():
    return pl.BlockSpec(memory_space=pltpu.SMEM)


def merge_pair(pair, scale):
    f32, width = jnp.float32, pair.shape[1]
    wide = jax.ShapeDtypeStruct((width, 2 * width), f32)
    return pl.pallas_call(
        functools.partial(pair_kernel, scale=scale),
        out_shape=(wide, jax.ShapeDtypeStruct((width, width), f32), wide),
        in_specs=[vmem()],
        out_specs=(vmem(),) * 3,
        scratch_shapes=[
            pltpu.VMEM((2 * width, 2 * width), f32),
            pltpu.VMEM((width, 2 * width), f32),
            pltpu.VMEM((width, 2 * width), f32),
            pltpu.VMEM((width, 2 * width), f32),
            pltpu.VMEM((width, width), f32),
            pltpu.VMEM((width, width), f32),
        ],
        compiler_params=pltpu.CompilerParams(vmem_limit_bytes=24 << 20),
        cost_estimate=pl.CostEstimate(flops=10**10, bytes_accessed=3 << 20, transcendentals=0),
        name="merge_pair",
    )(pair)


def cross_kernel(place_ref, mt_ref, inside_ref, mine_ref, other_ref, ahead_ref, seen_ref, x, *, scale):
    width = mt_ref.shape[0]
    snap, core = place_ref[0], place_ref[1]
    for k in range(2):
        for c in range(2):
            kept = mine_ref[(OWN + c) * width : (OWN + c + 1) * width]
            sent = other_ref[c * width : (c + 1) * width]
            rows = jnp.where(core == k, kept, sent)
            x[k * width : (k + 1) * width, c * width : (c + 1) * width] = rows * scale

    @pl.when(core == 0)
    def _():
        ahead_ref[...] = exact(mt_ref[...], x[...])

    @pl.when(core == 1)
    def _():
        ahead_ref[...] = exact(mt_ref[...], x[...], NT)

    for c in range(2):
        cols = slice(c * width, (c + 1) * width)

        @pl.when(snap == 2 * core + c)
        def _():
            seen_ref[...] = inside_ref[:, cols]

        @pl.when(snap == 2 - 2 * core + c)
        def _():
            seen_ref[...] = ahead_ref[:, cols]


def look_across(place, mt, inside, mine, other, scale):
    f32, width = jnp.float32, mt.shape[0]
    return pl.pallas_call(
        functools.partial(cross_kernel, scale=scale),
        out_shape=(jax.ShapeDtypeStruct((width, 2 * width), f32), jax.ShapeDtypeStruct((width, width), f32)),
        in_specs=[smem()] + [vmem()] * 4,
        out_specs=(vmem(),) * 2,
        scratch_shapes=[pltpu.VMEM((2 * width, 2 * width), f32)],
        compiler_params=pltpu.CompilerParams(vmem_limit_bytes=24 << 20),
        name="look_across",
    )(place, mt, inside, mine, other)


def root_kernel(
    place_ref, mt_ref, energy_ref, ahead_ref, seen_ref, mt2_ref, energy2_ref, ahead2_ref, seen2_ref, own_ref,
    modes_ref, coeffs_ref, g, pt, tt, small, li, h, mhi, mlo,
):
    width = mt_ref.shape[0]
    first, second = slice(0, width), slice(width, 2 * width)
    lower_core = place_ref[1] == 0
    of_pair = lambda k, a, b: jnp.where(lower_core, (a, b)[k][...], (a, b)[1 - k][...])
    mts = [of_pair(k, mt_ref, mt2_ref) for k in range(2)]
    cross = exact(of_pair(0, ahead_ref, ahead2_ref), mts[1], NT)
    g[first, first] = of_pair(0, energy_ref, energy2_ref)
    g[first, second] = cross
    g[second, first] = cross.T
    g[second, second] = of_pair(1, energy_ref, energy2_ref)
    pt[...] = g[first, :] + g[second, :]
    tt[...] = exact(pt[...], g[...])
    small[...] = exact(pt[...], tt[...], NT)
    for k in range(2):
        mhi[k], mlo[k] = split(mts[k])
        h[k * width : (k + 1) * width] = of_pair(k, seen_ref, seen2_ref)
    set_factor(small, li)
    pt[...] = exact(li[...], pt[...])
    coeffs_ref[...] = exact(pt[...], h[...])
    khi, klo = split(pt[...])
    share = own_ref.shape[1]
    step = min(share, 256)
    for r in range(share // step):
        rows = slice(r * step, (r + 1) * step)
        total = None
        for k in range(2):
            panel = None
            for b in range(2):
                cols = slice(b * width, (b + 1) * width)
                part = own_ref[2 * k + b, rows]
                term = single(part, mhi[k, :, cols], NT) + single(part, mlo[k, :, cols], NT)
                panel = term if panel is None else panel + term
            panel = panel.astype(jnp.bfloat16)
            cols = slice(k * width, (k + 1) * width)
            term = single(panel, khi[:, cols], NT) + single(panel, klo[:, cols], NT)
            total = term if total is None else total + term
        modes_ref[rows] = total


def merge_root(place, mine, other, own):
    f32 = jnp.float32
    width = own.shape[2]
    return pl.pallas_call(
        root_kernel,
        out_shape=(jax.ShapeDtypeStruct((own.shape[1], width), f32), jax.ShapeDtypeStruct((width, width), f32)),
        in_specs=[smem()] + [vmem()] * 9,
        out_specs=(vmem(),) * 2,
        scratch_shapes=[
            pltpu.VMEM((2 * width, 2 * width), f32),
            pltpu.VMEM((width, 2 * width), f32),
            pltpu.VMEM((width, 2 * width), f32),
            pltpu.VMEM((width, width), f32),
            pltpu.VMEM((width, width), f32),
            pltpu.VMEM((2 * width, width), f32),
            pltpu.VMEM((2, width, 2 * width), jnp.bfloat16),
            pltpu.VMEM((2, width, 2 * width), jnp.bfloat16),
        ],
        compiler_params=pltpu.CompilerParams(vmem_limit_bytes=40 << 20),
        name="merge_root",
    )(place, *mine, *other, own)


def gram_kernel(place_ref, own_ref, keep_ref, send_ref):
    width = own_ref.shape[2]
    for core, blocks in enumerate(HALVES):
        for k, (i, j) in enumerate(blocks):
            value = lax.dot_general(
                own_ref[i], own_ref[j], (((0,), (0,)), ((), ())), preferred_element_type=jnp.float32
            )
            rows = slice(k * width, (k + 1) * width)

            @pl.when(place_ref[1] == core)
            def _():
                keep_ref[rows] = value

            @pl.when(place_ref[1] != core)
            def _():
                send_ref[rows] = value


def gram_halves(place, own):
    width = own.shape[2]
    half = jax.ShapeDtypeStruct((len(HALVES[0]) * width, width), jnp.float32)
    return pl.pallas_call(
        gram_kernel,
        out_shape=(half, half),
        in_specs=[smem(), vmem()],
        out_specs=(vmem(),) * 2,
        compiler_params=pltpu.CompilerParams(vmem_limit_bytes=24 << 20),
        name="gram",
    )(place, own)


def swap_cores(value):
    return lax.ppermute(value, "core", [(0, 1), (1, 0)])


def sum_everywhere(part):
    rows, width = part.shape
    ring = lax.axis_size("x") * lax.axis_size("y")
    planes = lax.axis_size("z")
    piece = rows // ring
    part = lax.all_to_all(part.reshape(ring, piece, width), ("x", "y"), 0, 0).sum(0)
    part = lax.all_to_all(jnp.broadcast_to(part, (planes, piece, width)), "z", 0, 0).sum(0)
    return lax.all_to_all(jnp.broadcast_to(part, (ring, piece, width)), ("x", "y"), 0, 0).reshape(rows, width)


def on_device(snapshots):
    cell_rows, width = snapshots.shape
    n_snap = lax.axis_size("y")
    share = cell_rows // n_snap
    cells = cell_rows * lax.axis_size("z") * lax.axis_size("x") * lax.axis_size("core")
    scale = 1.0 / cells
    place = jnp.stack([lax.axis_index("y"), lax.axis_index("core")]).astype(jnp.int32)
    own = lax.all_to_all(snapshots.reshape(n_snap, share, width), "y", 0, 0)
    keep, send = gram_halves(place, own)
    half = sum_everywhere(keep + swap_cores(send))
    other = swap_cores(half[OWN * width :])
    mt, energy, inside = merge_pair(half, scale)
    ahead, seen = look_across(place, mt, inside, half, other, scale)
    mine = (mt, energy, ahead, seen)
    return merge_root(place, mine, [swap_cores(value) for value in mine], own)


def solution(mesh):
    n_cell, n_snap = mesh.devices.shape
    cores, across = 2, 4
    fine = Mesh(
        mesh.devices.reshape(n_cell // (cores * across), across, cores, n_snap), ("z", "x", "core", "y")
    )
    cell = ("z", "x", "core")
    return jax.shard_map(
        on_device,
        mesh=fine,
        in_specs=(P(cell, "y"),),
        out_specs=(P(cell + ("y",), None), P(None, "y")),
        check_vma=False,
    )
```

```python
import functools
import math
import jax
import jax.numpy as jnp
from jax import lax
from jax.experimental import pallas as pl
from jax.experimental.pallas import tpu as pltpu
from jax.sharding import Mesh, PartitionSpec as P

HI = lax.Precision.HIGHEST
HALVES = (((0, 1), (0, 2), (0, 3)), ((2, 3), (1, 2), (1, 3)))
TN = (((0,), (0,)), ((), ()))
NN = (((1,), (0,)), ((), ()))
NT = (((1,), (1,)), ((), ()))
EDGE = 128


def exact(a, b, dims=NN):
    return lax.dot_general(a, b, dims, precision=HI, preferred_element_type=jnp.float32)


def split(a):
    high = a.astype(jnp.bfloat16)
    return high, (a - high.astype(jnp.float32)).astype(jnp.bfloat16)


def single(a, b, dims=NN):
    return lax.dot_general(a, b, dims, preferred_element_type=jnp.float32)


def eliminate(block, ahead=6):
    tiles = EDGE // 8
    sub = lax.broadcasted_iota(jnp.int32, (8, EDGE), 0)
    lane = lax.broadcasted_iota(jnp.int32, (8, EDGE), 1)
    spread = lambda value: jnp.broadcast_to(value, (8, EDGE))
    rows = [block[8 * u : 8 * u + 8] for u in range(tiles)]
    cols = {c: [spread(rows[u][:, c : c + 1]) for u in range(tiles)] for c in range(ahead)}
    pivots = [None] * tiles
    for j in range(EDGE):
        t, s = divmod(j, 8)
        col = cols.pop(j)
        pivot = spread(col[t][s : s + 1, :])
        inverse = 1.0 / pivot
        pivots[t] = pivot if s == 0 else jnp.where(sub >= s, pivot, pivots[t])
        factor = [None] * tiles
        for u in range(t, tiles):
            factor[u] = (jnp.where(sub > s, col[u], 0.0) if u == t else col[u]) * inverse
        for c in range(j + 1, min(j + ahead, EDGE)):
            entry = spread(cols[c][t][s : s + 1, :])
            cols[c] = [None if u < t else cols[c][u] - factor[u] * entry for u in range(tiles)]
        row = jnp.where(lane == j, 1.0, spread(rows[t][s : s + 1, :]))
        for u in range(t, tiles):
            value = jnp.where(lane == j, 0.0, rows[u]) - factor[u] * row
            rows[u] = jnp.where(sub > s, value, rows[u]) if u == t else value
        c = j + ahead
        if c < EDGE:
            cols[c] = [None if u < t else spread(rows[u][:, c : c + 1]) for u in range(tiles)]
    scale = [lax.rsqrt(p) for p in pivots]
    upper, inverse = [], []
    for u in range(tiles):
        at = sub + 8 * u
        upper.append(jnp.where(lane >= at, rows[u], 0.0) * scale[u])
        inverse.append(jnp.where(lane < at, rows[u], jnp.where(lane == at, 1.0, 0.0)) * scale[u])
    return jnp.concatenate(upper, 0), jnp.concatenate(inverse, 0)


def set_factor(gram, inverse):
    n = EDGE
    top, bottom = slice(0, n), slice(n, 2 * n)
    _, head = eliminate(gram[top, top])
    low = exact(gram[bottom, top], head, NT)
    _, tail = eliminate(gram[bottom, bottom] - exact(low, low, NT))
    inverse[top, top] = head
    inverse[top, bottom] = jnp.zeros((n, n), jnp.float32)
    inverse[bottom, bottom] = tail
    inverse[bottom, top] = -exact(tail, exact(low, head))


def set_lower(gram, lower):
    n = EDGE
    top, bottom = slice(0, n), slice(n, 2 * n)
    upper, head = eliminate(gram[top, top])
    low = exact(gram[bottom, top], head, NT)
    tail, _ = eliminate(gram[bottom, bottom] - exact(low, low, NT))
    lower[top, top] = upper.T
    lower[top, bottom] = jnp.zeros((n, n), jnp.float32)
    lower[bottom, top] = low
    lower[bottom, bottom] = tail.T


def pair_kernel(place_ref, half_ref, diag_ref, mt_ref, energy_ref, inside_ref, g, pt, tt, wt, small, li, *, scale):
    width = half_ref.shape[2]
    first, second = slice(0, width), slice(width, 2 * width)
    core = place_ref[1]
    snaps, across = 4, half_ref.shape[0] // 4
    off = len(HALVES[0]) * width // half_ref.shape[0]
    unit = half_ref.shape[1] - off
    step = math.gcd(off, width)
    for r in range(0, width, step):
        g[r : r + step, second] = half_ref[r // off, r % off : r % off + step] * scale
    g[second, first] = g[first, second].T
    for k in range(2):
        cols = slice(k * width, (k + 1) * width)
        for mine in range(2):

            @pl.when(core == mine)
            def _():
                for a in range(across):
                    to = k * width + (2 * a + mine) * unit
                    g[to : to + unit, cols] = half_ref[a * snaps + 2 * mine + k, off:] * scale
                    to = k * width + (2 * a + 1 - mine) * unit
                    g[to : to + unit, cols] = diag_ref[k, a * unit : (a + 1) * unit] * scale

    pt[...] = g[first, :] + g[second, :]
    tt[...] = exact(pt[...], g[...])
    small[...] = exact(pt[...], tt[...], NT)
    set_factor(small, li)
    wt[...] = exact(li[...], tt[...])
    pt[...] = exact(li[...], pt[...])
    energy_ref[...] = exact(wt[...], wt[...], NT)
    set_lower(energy_ref, li)
    mt_ref[...] = exact(li[...], pt[...])
    inside_ref[...] = exact(li[...], wt[...])


def vmem():
    return pl.BlockSpec(memory_space=pltpu.VMEM)


def smem():
    return pl.BlockSpec(memory_space=pltpu.SMEM)


def merge_pair(place, half, diag, scale):
    f32, width = jnp.float32, half.shape[2]
    wide = jax.ShapeDtypeStruct((width, 2 * width), f32)
    return pl.pallas_call(
        functools.partial(pair_kernel, scale=scale),
        out_shape=(wide, jax.ShapeDtypeStruct((width, width), f32), wide),
        in_specs=[smem(), vmem(), vmem()],
        out_specs=(vmem(),) * 3,
        scratch_shapes=[
            pltpu.VMEM((2 * width, 2 * width), f32),
            pltpu.VMEM((width, 2 * width), f32),
            pltpu.VMEM((width, 2 * width), f32),
            pltpu.VMEM((width, 2 * width), f32),
            pltpu.VMEM((width, width), f32),
            pltpu.VMEM((width, width), f32),
        ],
        compiler_params=pltpu.CompilerParams(vmem_limit_bytes=24 << 20),
        cost_estimate=pl.CostEstimate(flops=10**10, bytes_accessed=3 << 20, transcendentals=0),
        name="merge_pair",
    )(place, half, diag)


def cross_kernel(place_ref, mt_ref, inside_ref, mine_ref, other_ref, ahead_ref, seen_ref, x, *, scale):
    width = mt_ref.shape[0]
    snap, core = place_ref[0], place_ref[1]
    for k in range(2):
        for c in range(2):
            rows = slice(c * width, (c + 1) * width)
            rows = jnp.where(core == k, mine_ref[rows], other_ref[rows])
            x[k * width : (k + 1) * width, c * width : (c + 1) * width] = rows * scale

    @pl.when(core == 0)
    def _():
        ahead_ref[...] = exact(mt_ref[...], x[...])

    @pl.when(core == 1)
    def _():
        ahead_ref[...] = exact(mt_ref[...], x[...], NT)

    for c in range(2):
        cols = slice(c * width, (c + 1) * width)

        @pl.when(snap == 2 * core + c)
        def _():
            seen_ref[...] = inside_ref[:, cols]

        @pl.when(snap == 2 - 2 * core + c)
        def _():
            seen_ref[...] = ahead_ref[:, cols]


def look_across(place, mt, inside, mine, other, scale):
    f32, width = jnp.float32, mt.shape[0]
    return pl.pallas_call(
        functools.partial(cross_kernel, scale=scale),
        out_shape=(jax.ShapeDtypeStruct((width, 2 * width), f32), jax.ShapeDtypeStruct((width, width), f32)),
        in_specs=[smem()] + [vmem()] * 4,
        out_specs=(vmem(),) * 2,
        scratch_shapes=[pltpu.VMEM((2 * width, 2 * width), f32)],
        compiler_params=pltpu.CompilerParams(vmem_limit_bytes=24 << 20),
        name="look_across",
    )(place, mt, inside, mine, other)


def root_kernel(
    place_ref, mt_ref, energy_ref, ahead_ref, seen_ref, mt2_ref, energy2_ref, ahead2_ref, seen2_ref, own_ref,
    modes_ref, coeffs_ref, g, pt, tt, small, li, h, mhi, mlo,
):
    width = mt_ref.shape[0]
    first, second = slice(0, width), slice(width, 2 * width)
    lower_core = place_ref[1] == 0
    of_pair = lambda k, a, b: jnp.where(lower_core, (a, b)[k][...], (a, b)[1 - k][...])
    mts = [of_pair(k, mt_ref, mt2_ref) for k in range(2)]
    cross = exact(of_pair(0, ahead_ref, ahead2_ref), mts[1], NT)
    g[first, first] = of_pair(0, energy_ref, energy2_ref)
    g[first, second] = cross
    g[second, first] = cross.T
    g[second, second] = of_pair(1, energy_ref, energy2_ref)
    pt[...] = g[first, :] + g[second, :]
    tt[...] = exact(pt[...], g[...])
    small[...] = exact(pt[...], tt[...], NT)
    for k in range(2):
        mhi[k], mlo[k] = split(mts[k])
        h[k * width : (k + 1) * width] = of_pair(k, seen_ref, seen2_ref)
    set_factor(small, li)
    pt[...] = exact(li[...], pt[...])
    coeffs_ref[...] = exact(pt[...], h[...])
    khi, klo = split(pt[...])
    share = own_ref.shape[1]
    step = min(share, 256)
    for r in range(share // step):
        rows = slice(r * step, (r + 1) * step)
        total = None
        for k in range(2):
            panel = None
            for b in range(2):
                cols = slice(b * width, (b + 1) * width)
                part = own_ref[2 * k + b, rows]
                term = single(part, mhi[k, :, cols], NT) + single(part, mlo[k, :, cols], NT)
                panel = term if panel is None else panel + term
            panel = panel.astype(jnp.bfloat16)
            cols = slice(k * width, (k + 1) * width)
            term = single(panel, khi[:, cols], NT) + single(panel, klo[:, cols], NT)
            total = term if total is None else total + term
        modes_ref[rows] = total


def merge_root(place, mine, other, own):
    f32 = jnp.float32
    width = own.shape[2]
    return pl.pallas_call(
        root_kernel,
        out_shape=(jax.ShapeDtypeStruct((own.shape[1], width), f32), jax.ShapeDtypeStruct((width, width), f32)),
        in_specs=[smem()] + [vmem()] * 9,
        out_specs=(vmem(),) * 2,
        scratch_shapes=[
            pltpu.VMEM((2 * width, 2 * width), f32),
            pltpu.VMEM((width, 2 * width), f32),
            pltpu.VMEM((width, 2 * width), f32),
            pltpu.VMEM((width, width), f32),
            pltpu.VMEM((width, width), f32),
            pltpu.VMEM((2 * width, width), f32),
            pltpu.VMEM((2, width, 2 * width), jnp.bfloat16),
            pltpu.VMEM((2, width, 2 * width), jnp.bfloat16),
        ],
        compiler_params=pltpu.CompilerParams(vmem_limit_bytes=40 << 20),
        name="merge_root",
    )(place, *mine, *other, own)


def cross_gram_kernel(place_ref, here_ref, below_ref, far_ref, far2_ref, above_ref, after_ref, own_ref, keep_ref, send_ref):
    share, width = here_ref.shape
    for k, ref in ((0, here_ref), (3, below_ref), (1, above_ref)):
        own_ref[lax.rem(place_ref[0] + k, 4)] = ref[:share]
    for k, ref in enumerate((far_ref, far2_ref)):
        own_ref[lax.rem(place_ref[0] + 2, 4), k * share // 2 : (k + 1) * share // 2] = ref[...]
    for i in range(3):
        right = jnp.concatenate([own_ref[j] for j in range(i + 1, 4)], 1)
        wide = lax.dot_general(own_ref[i], right, TN, preferred_element_type=jnp.float32)
        for j in range(i + 1, 4):
            value = wide[:, (j - i - 1) * width : (j - i) * width]
            for core in range(2):
                if (i, j) not in HALVES[core]:
                    continue
                rows = slice(HALVES[core].index((i, j)) * width, (HALVES[core].index((i, j)) + 1) * width)

                @pl.when(place_ref[1] == core)
                def _():
                    keep_ref[rows] = value

                @pl.when(place_ref[1] != core)
                def _():
                    send_ref[rows] = value


def cross_gram(place, owns, after):
    share, width = owns[0].shape
    half = jax.ShapeDtypeStruct((len(HALVES[0]) * width, width), jnp.float32)
    return pl.pallas_call(
        cross_gram_kernel,
        out_shape=(jax.ShapeDtypeStruct((4, share, width), owns[0].dtype), half, half),
        in_specs=[smem()] + [vmem()] * 5 + [pl.BlockSpec(memory_space=pl.ANY)],
        out_specs=(vmem(),) * 3,
        compiler_params=pltpu.CompilerParams(vmem_limit_bytes=24 << 20),
        name="cross_gram",
    )(place, *owns, after)


def own_gram_kernel(snap_ref, *refs):
    refs[-1][...] = lax.dot_general(snap_ref[...], snap_ref[...], TN, preferred_element_type=jnp.float32)


def own_gram(snapshots, after):
    width = snapshots.shape[1]
    return pl.pallas_call(
        own_gram_kernel,
        out_shape=jax.ShapeDtypeStruct((width, width), jnp.float32),
        in_specs=[vmem()] + [pl.BlockSpec(memory_space=pl.ANY)] * len(after),
        out_specs=vmem(),
        compiler_params=pltpu.CompilerParams(vmem_limit_bytes=24 << 20),
        name="own_gram",
    )(snapshots, *after)


def swap_cores(value):
    return lax.ppermute(value, "core", [(0, 1), (1, 0)])


def gather_sum(part, axes):
    rows, width = part.shape
    ring = lax.axis_size(axes)
    return lax.all_to_all(part.reshape(ring, rows // ring, width), axes, 0, 0).sum(0)


def sum_planes(piece):
    planes = lax.axis_size("z")
    return lax.all_to_all(jnp.broadcast_to(piece, (planes,) + piece.shape), "z", 0, 0).sum(0)


def on_device(snapshots):
    cell_rows, width = snapshots.shape
    n_snap = lax.axis_size("y")
    share = cell_rows // n_snap
    cells = cell_rows * lax.axis_size("z") * lax.axis_size("x") * lax.axis_size("core")
    scale = 1.0 / cells
    snap, core = lax.axis_index("y"), lax.axis_index("core")
    place = jnp.stack([snap, core]).astype(jnp.int32)
    cut = lambda k, start, rows: lax.dynamic_slice_in_dim(
        snapshots, lax.rem(snap + k, n_snap) * share + start, rows, 0
    )
    relay = share // 2
    right = jnp.concatenate([cut(1, 0, share), cut(2, 0, relay)], 0)
    left = jnp.concatenate([cut(3, 0, share), cut(2, relay, relay)], 0)
    ahead = [(i, (i + 1) % n_snap) for i in range(n_snap)]
    back = [(i, (i - 1) % n_snap) for i in range(n_snap)]
    below, above = lax.ppermute(right, "y", ahead), lax.ppermute(left, "y", back)
    owns = (
        cut(0, 0, share),
        below,
        lax.ppermute(below[share:], "y", ahead),
        lax.ppermute(above[share:], "y", back),
        above,
    )
    diag_piece = gather_sum(own_gram(snapshots, (right, left)), "x").reshape(2, -1, width)
    keep, send = (lax.dynamic_index_in_dim(diag_piece, c, 0, keepdims=False) for c in (core, 1 - core))
    diag_piece = sum_planes(keep + swap_cores(send))
    own, keep, send = cross_gram(place, owns, diag_piece)
    piece = sum_planes(gather_sum(keep + swap_cores(send), ("x", "y")))
    off = piece.shape[0]
    piece = jnp.concatenate([piece, diag_piece], 0)
    ring = lax.axis_size(("x", "y"))
    half = lax.all_to_all(jnp.broadcast_to(piece, (ring,) + piece.shape), ("x", "y"), 0, 0)
    diag = half[:, off:].reshape(ring // n_snap, 2, 2, -1, width)
    diag = lax.dynamic_index_in_dim(diag, 1 - core, 1, keepdims=False).transpose(1, 0, 2, 3)
    diag = swap_cores(diag.reshape(2, width // 2, width))
    cross = half[:, :off].reshape(ring * off, width)[width:]
    mt, energy, inside = merge_pair(place, half, diag, scale)
    ahead, seen = look_across(place, mt, inside, cross, swap_cores(cross), scale)
    mine = (mt, energy, ahead, seen)
    return merge_root(place, mine, [swap_cores(value) for value in mine], own)


def solution(mesh):
    n_cell, n_snap = mesh.devices.shape
    cores, across = 2, 4
    fine = Mesh(
        mesh.devices.reshape(n_cell // (cores * across), across, cores, n_snap), ("z", "x", "core", "y")
    )
    cell = ("z", "x", "core")
    return jax.shard_map(
        on_device,
        mesh=fine,
        in_specs=(P(cell, "y"),),
        out_specs=(P(cell + ("y",), None), P(None, "y")),
        check_vma=False,
    )
```

```python
import functools
import math
import jax
import jax.numpy as jnp
from jax import lax
from jax.experimental import pallas as pl
from jax.experimental.pallas import tpu as pltpu
from jax.sharding import Mesh, PartitionSpec as P

HI = lax.Precision.HIGHEST
HALVES = (((0, 1), (0, 2), (0, 3)), ((2, 3), (1, 2), (1, 3)))
TN = (((0,), (0,)), ((), ()))
NN = (((1,), (0,)), ((), ()))
NT = (((1,), (1,)), ((), ()))
EDGE = 128


def exact(a, b, dims=NN):
    return lax.dot_general(a, b, dims, precision=HI, preferred_element_type=jnp.float32)


def split(a):
    high = a.astype(jnp.bfloat16)
    return high, (a - high.astype(jnp.float32)).astype(jnp.bfloat16)


def single(a, b, dims=NN):
    return lax.dot_general(a, b, dims, preferred_element_type=jnp.float32)


def eliminate(block, ahead=6):
    tiles = EDGE // 8
    sub = lax.broadcasted_iota(jnp.int32, (8, EDGE), 0)
    lane = lax.broadcasted_iota(jnp.int32, (8, EDGE), 1)
    spread = lambda value: jnp.broadcast_to(value, (8, EDGE))
    rows = [block[8 * u : 8 * u + 8] for u in range(tiles)]
    cols = {c: [spread(rows[u][:, c : c + 1]) for u in range(tiles)] for c in range(ahead)}
    pivots = [None] * tiles
    for j in range(EDGE):
        t, s = divmod(j, 8)
        col = cols.pop(j)
        pivot = spread(col[t][s : s + 1, :])
        inverse = 1.0 / pivot
        pivots[t] = pivot if s == 0 else jnp.where(sub >= s, pivot, pivots[t])
        factor = [None] * tiles
        for u in range(t, tiles):
            factor[u] = (jnp.where(sub > s, col[u], 0.0) if u == t else col[u]) * inverse
        for c in range(j + 1, min(j + ahead, EDGE)):
            entry = spread(cols[c][t][s : s + 1, :])
            cols[c] = [None if u < t else cols[c][u] - factor[u] * entry for u in range(tiles)]
        row = jnp.where(lane == j, 1.0, spread(rows[t][s : s + 1, :]))
        for u in range(t, tiles):
            value = jnp.where(lane == j, 0.0, rows[u]) - factor[u] * row
            rows[u] = jnp.where(sub > s, value, rows[u]) if u == t else value
        c = j + ahead
        if c < EDGE:
            cols[c] = [None if u < t else spread(rows[u][:, c : c + 1]) for u in range(tiles)]
    scale = [lax.rsqrt(p) for p in pivots]
    upper, inverse = [], []
    for u in range(tiles):
        at = sub + 8 * u
        upper.append(jnp.where(lane >= at, rows[u], 0.0) * scale[u])
        inverse.append(jnp.where(lane < at, rows[u], jnp.where(lane == at, 1.0, 0.0)) * scale[u])
    return jnp.concatenate(upper, 0), jnp.concatenate(inverse, 0)


def set_factor(gram, inverse):
    n = EDGE
    top, bottom = slice(0, n), slice(n, 2 * n)
    _, head = eliminate(gram[top, top])
    low = exact(gram[bottom, top], head, NT)
    _, tail = eliminate(gram[bottom, bottom] - exact(low, low, NT))
    inverse[top, top] = head
    inverse[top, bottom] = jnp.zeros((n, n), jnp.float32)
    inverse[bottom, bottom] = tail
    inverse[bottom, top] = -exact(tail, exact(low, head))


def set_lower(gram, lower):
    n = EDGE
    top, bottom = slice(0, n), slice(n, 2 * n)
    upper, head = eliminate(gram[top, top])
    low = exact(gram[bottom, top], head, NT)
    tail, _ = eliminate(gram[bottom, bottom] - exact(low, low, NT))
    lower[top, top] = upper.T
    lower[top, bottom] = jnp.zeros((n, n), jnp.float32)
    lower[bottom, top] = low
    lower[bottom, bottom] = tail.T


def pair_kernel(place_ref, half_ref, diag_ref, mt_ref, energy_ref, inside_ref, g, pt, tt, wt, small, li, *, scale):
    width = half_ref.shape[2]
    first, second = slice(0, width), slice(width, 2 * width)
    core = place_ref[1]
    snaps, across = 4, half_ref.shape[0] // 4
    off = len(HALVES[0]) * width // half_ref.shape[0]
    unit = half_ref.shape[1] - off
    step = math.gcd(off, width)
    for r in range(0, width, step):
        g[r : r + step, second] = half_ref[r // off, r % off : r % off + step] * scale
    g[second, first] = g[first, second].T
    for k in range(2):
        cols = slice(k * width, (k + 1) * width)
        for mine in range(2):

            @pl.when(core == mine)
            def _():
                for a in range(across):
                    to = k * width + (2 * a + mine) * unit
                    g[to : to + unit, cols] = half_ref[a * snaps + 2 * mine + k, off:] * scale
                    to = k * width + (2 * a + 1 - mine) * unit
                    g[to : to + unit, cols] = diag_ref[k, a * unit : (a + 1) * unit] * scale

    pt[...] = g[first, :] + g[second, :]
    tt[...] = exact(pt[...], g[...])
    small[...] = exact(pt[...], tt[...], NT)
    set_factor(small, li)
    wt[...] = exact(li[...], tt[...])
    pt[...] = exact(li[...], pt[...])
    energy_ref[...] = exact(wt[...], wt[...], NT)
    set_lower(energy_ref, li)
    mt_ref[...] = exact(li[...], pt[...])
    inside_ref[...] = exact(li[...], wt[...])


def vmem():
    return pl.BlockSpec(memory_space=pltpu.VMEM)


def smem():
    return pl.BlockSpec(memory_space=pltpu.SMEM)


def merge_pair(place, half, diag, scale):
    f32, width = jnp.float32, half.shape[2]
    wide = jax.ShapeDtypeStruct((width, 2 * width), f32)
    return pl.pallas_call(
        functools.partial(pair_kernel, scale=scale),
        out_shape=(wide, jax.ShapeDtypeStruct((width, width), f32), wide),
        in_specs=[smem(), vmem(), vmem()],
        out_specs=(vmem(),) * 3,
        scratch_shapes=[
            pltpu.VMEM((2 * width, 2 * width), f32),
            pltpu.VMEM((width, 2 * width), f32),
            pltpu.VMEM((width, 2 * width), f32),
            pltpu.VMEM((width, 2 * width), f32),
            pltpu.VMEM((width, width), f32),
            pltpu.VMEM((width, width), f32),
        ],
        compiler_params=pltpu.CompilerParams(vmem_limit_bytes=24 << 20),
        cost_estimate=pl.CostEstimate(flops=10**10, bytes_accessed=3 << 20, transcendentals=0),
        name="merge_pair",
    )(place, half, diag)


def cross_kernel(place_ref, mt_ref, inside_ref, mine_ref, other_ref, ahead_ref, seen_ref, x, *, scale):
    width = mt_ref.shape[0]
    snap, core = place_ref[0], place_ref[1]
    for k in range(2):
        for c in range(2):
            rows = slice(c * width, (c + 1) * width)
            rows = jnp.where(core == k, mine_ref[rows], other_ref[rows])
            x[k * width : (k + 1) * width, c * width : (c + 1) * width] = rows * scale

    @pl.when(core == 0)
    def _():
        ahead_ref[...] = exact(mt_ref[...], x[...])

    @pl.when(core == 1)
    def _():
        ahead_ref[...] = exact(mt_ref[...], x[...], NT)

    for c in range(2):
        cols = slice(c * width, (c + 1) * width)

        @pl.when(snap == 2 * core + c)
        def _():
            seen_ref[...] = inside_ref[:, cols]

        @pl.when(snap == 2 - 2 * core + c)
        def _():
            seen_ref[...] = ahead_ref[:, cols]


def look_across(place, mt, inside, mine, other, scale):
    f32, width = jnp.float32, mt.shape[0]
    return pl.pallas_call(
        functools.partial(cross_kernel, scale=scale),
        out_shape=(jax.ShapeDtypeStruct((width, 2 * width), f32), jax.ShapeDtypeStruct((width, width), f32)),
        in_specs=[smem()] + [vmem()] * 4,
        out_specs=(vmem(),) * 2,
        scratch_shapes=[pltpu.VMEM((2 * width, 2 * width), f32)],
        compiler_params=pltpu.CompilerParams(vmem_limit_bytes=24 << 20),
        name="look_across",
    )(place, mt, inside, mine, other)


def root_kernel(
    place_ref, mt_ref, energy_ref, ahead_ref, seen_ref, mt2_ref, energy2_ref, ahead2_ref, seen2_ref, own_ref,
    modes_ref, coeffs_ref, g, pt, tt, small, li, h, mhi, mlo,
):
    width = mt_ref.shape[0]
    first, second = slice(0, width), slice(width, 2 * width)
    lower_core = place_ref[1] == 0
    of_pair = lambda k, a, b: jnp.where(lower_core, (a, b)[k][...], (a, b)[1 - k][...])
    mts = [of_pair(k, mt_ref, mt2_ref) for k in range(2)]
    cross = exact(of_pair(0, ahead_ref, ahead2_ref), mts[1], NT)
    g[first, first] = of_pair(0, energy_ref, energy2_ref)
    g[first, second] = cross
    g[second, first] = cross.T
    g[second, second] = of_pair(1, energy_ref, energy2_ref)
    pt[...] = g[first, :] + g[second, :]
    tt[...] = exact(pt[...], g[...])
    small[...] = exact(pt[...], tt[...], NT)
    for k in range(2):
        mhi[k], mlo[k] = split(mts[k])
        h[k * width : (k + 1) * width] = of_pair(k, seen_ref, seen2_ref)
    set_factor(small, li)
    pt[...] = exact(li[...], pt[...])
    coeffs_ref[...] = exact(pt[...], h[...])
    khi, klo = split(pt[...])
    share = own_ref.shape[1]
    step = min(share, 256)
    for r in range(share // step):
        rows = slice(r * step, (r + 1) * step)
        total = None
        for k in range(2):
            panel = None
            for b in range(2):
                cols = slice(b * width, (b + 1) * width)
                part = own_ref[2 * k + b, rows]
                term = single(part, mhi[k, :, cols], NT) + single(part, mlo[k, :, cols], NT)
                panel = term if panel is None else panel + term
            panel = panel.astype(jnp.bfloat16)
            cols = slice(k * width, (k + 1) * width)
            term = single(panel, khi[:, cols], NT) + single(panel, klo[:, cols], NT)
            total = term if total is None else total + term
        modes_ref[rows] = total


def merge_root(place, mine, other, own):
    f32 = jnp.float32
    width = own.shape[2]
    return pl.pallas_call(
        root_kernel,
        out_shape=(jax.ShapeDtypeStruct((own.shape[1], width), f32), jax.ShapeDtypeStruct((width, width), f32)),
        in_specs=[smem()] + [vmem()] * 9,
        out_specs=(vmem(),) * 2,
        scratch_shapes=[
            pltpu.VMEM((2 * width, 2 * width), f32),
            pltpu.VMEM((width, 2 * width), f32),
            pltpu.VMEM((width, 2 * width), f32),
            pltpu.VMEM((width, width), f32),
            pltpu.VMEM((width, width), f32),
            pltpu.VMEM((2 * width, width), f32),
            pltpu.VMEM((2, width, 2 * width), jnp.bfloat16),
            pltpu.VMEM((2, width, 2 * width), jnp.bfloat16),
        ],
        compiler_params=pltpu.CompilerParams(vmem_limit_bytes=40 << 20),
        name="merge_root",
    )(place, *mine, *other, own)


def cross_gram_kernel(place_ref, own_ref, after_ref, keep_ref, send_ref):
    width = own_ref.shape[2]
    for i in range(3):
        right = jnp.concatenate([own_ref[j] for j in range(i + 1, 4)], 1)
        wide = lax.dot_general(own_ref[i], right, TN, preferred_element_type=jnp.float32)
        for j in range(i + 1, 4):
            value = wide[:, (j - i - 1) * width : (j - i) * width]
            for core in range(2):
                if (i, j) not in HALVES[core]:
                    continue
                rows = slice(HALVES[core].index((i, j)) * width, (HALVES[core].index((i, j)) + 1) * width)

                @pl.when(place_ref[1] == core)
                def _():
                    keep_ref[rows] = value

                @pl.when(place_ref[1] != core)
                def _():
                    send_ref[rows] = value


def cross_gram(place, own, after):
    width = own.shape[2]
    half = jax.ShapeDtypeStruct((len(HALVES[0]) * width, width), jnp.float32)
    return pl.pallas_call(
        cross_gram_kernel,
        out_shape=(half, half),
        in_specs=[smem(), vmem(), pl.BlockSpec(memory_space=pl.ANY)],
        out_specs=(vmem(),) * 2,
        compiler_params=pltpu.CompilerParams(vmem_limit_bytes=24 << 20),
        name="cross_gram",
    )(place, own, after)


def own_gram_kernel(snap_ref, gram_ref):
    gram_ref[...] = lax.dot_general(snap_ref[...], snap_ref[...], TN, preferred_element_type=jnp.float32)


def own_gram(snapshots):
    width = snapshots.shape[1]
    return pl.pallas_call(
        own_gram_kernel,
        out_shape=jax.ShapeDtypeStruct((width, width), jnp.float32),
        in_specs=[vmem()],
        out_specs=vmem(),
        compiler_params=pltpu.CompilerParams(vmem_limit_bytes=24 << 20),
        name="own_gram",
    )(snapshots)


def swap_cores(value):
    return lax.ppermute(value, "core", [(0, 1), (1, 0)])


def gather_sum(part, axes):
    rows, width = part.shape
    ring = lax.axis_size(axes)
    return lax.all_to_all(part.reshape(ring, rows // ring, width), axes, 0, 0).sum(0)


def sum_planes(piece):
    planes = lax.axis_size("z")
    return lax.all_to_all(jnp.broadcast_to(piece, (planes,) + piece.shape), "z", 0, 0).sum(0)


def sum_own_gram(gram, core):
    across, planes = lax.axis_size("x"), lax.axis_size("z")
    place = lax.axis_index("x")
    piece = gram.shape[0] // across
    cut = lambda k: lax.dynamic_slice_in_dim(gram, lax.rem(place + k, across) * piece, piece, 0)
    total = cut(0)
    for part in [lax.ppermute(cut(k), "x", [(i, (i + k) % across) for i in range(across)]) for k in range(1, across)]:
        total = total + part
    total = total.reshape(2, piece // 2, -1)
    keep, send = (lax.dynamic_index_in_dim(total, c, 0, keepdims=False) for c in (core, 1 - core))
    total = keep + swap_cores(send)
    bit = 1
    while bit < planes:
        before = total
        total = total + lax.ppermute(total, "z", [(i, i ^ bit) for i in range(planes)])
        bit *= 2
    return before, total


def on_device(snapshots):
    cell_rows, width = snapshots.shape
    n_snap = lax.axis_size("y")
    share = cell_rows // n_snap
    cells = cell_rows * lax.axis_size("z") * lax.axis_size("x") * lax.axis_size("core")
    scale = 1.0 / cells
    snap, core = lax.axis_index("y"), lax.axis_index("core")
    place = jnp.stack([snap, core]).astype(jnp.int32)
    own = lax.all_to_all(snapshots.reshape(n_snap, share, width), "y", 0, 0)
    before, diag_piece = sum_own_gram(own_gram(snapshots), core)
    keep, send = cross_gram(place, own, before)
    piece = sum_planes(gather_sum(keep + swap_cores(send), ("x", "y")))
    off = piece.shape[0]
    piece = jnp.concatenate([piece, diag_piece], 0)
    ring = lax.axis_size(("x", "y"))
    half = lax.all_to_all(jnp.broadcast_to(piece, (ring,) + piece.shape), ("x", "y"), 0, 0)
    diag = half[:, off:].reshape(ring // n_snap, 2, 2, -1, width)
    diag = lax.dynamic_index_in_dim(diag, 1 - core, 1, keepdims=False).transpose(1, 0, 2, 3)
    diag = swap_cores(diag.reshape(2, width // 2, width))
    cross = half[:, :off].reshape(ring * off, width)[width:]
    mt, energy, inside = merge_pair(place, half, diag, scale)
    ahead, seen = look_across(place, mt, inside, cross, swap_cores(cross), scale)
    mine = (mt, energy, ahead, seen)
    return merge_root(place, mine, [swap_cores(value) for value in mine], own)


def solution(mesh):
    n_cell, n_snap = mesh.devices.shape
    cores, across = 2, 4
    fine = Mesh(
        mesh.devices.reshape(n_cell // (cores * across), across, cores, n_snap), ("z", "x", "core", "y")
    )
    cell = ("z", "x", "core")
    return jax.shard_map(
        on_device,
        mesh=fine,
        in_specs=(P(cell, "y"),),
        out_specs=(P(cell + ("y",), None), P(None, "y")),
        check_vma=False,
    )
```

```python
import functools
import math
import jax
import jax.numpy as jnp
from jax import lax
from jax.experimental import pallas as pl
from jax.experimental.pallas import tpu as pltpu
from jax.sharding import Mesh, PartitionSpec as P

HI = lax.Precision.HIGHEST
HALVES = (((0, 1), (0, 2), (0, 3)), ((2, 3), (1, 2), (1, 3)))
TN = (((0,), (0,)), ((), ()))
NN = (((1,), (0,)), ((), ()))
NT = (((1,), (1,)), ((), ()))
EDGE = 128


def exact(a, b, dims=NN):
    return lax.dot_general(a, b, dims, precision=HI, preferred_element_type=jnp.float32)


def split(a):
    high = a.astype(jnp.bfloat16)
    return high, (a - high.astype(jnp.float32)).astype(jnp.bfloat16)


def single(a, b, dims=NN):
    return lax.dot_general(a, b, dims, preferred_element_type=jnp.float32)


def eliminate(block, ahead=6):
    tiles = EDGE // 8
    sub = lax.broadcasted_iota(jnp.int32, (8, EDGE), 0)
    lane = lax.broadcasted_iota(jnp.int32, (8, EDGE), 1)
    spread = lambda value: jnp.broadcast_to(value, (8, EDGE))
    rows = [block[8 * u : 8 * u + 8] for u in range(tiles)]
    cols = {c: [spread(rows[u][:, c : c + 1]) for u in range(tiles)] for c in range(ahead)}
    pivots = [None] * tiles
    for j in range(EDGE):
        t, s = divmod(j, 8)
        col = cols.pop(j)
        pivot = spread(col[t][s : s + 1, :])
        inverse = 1.0 / pivot
        pivots[t] = pivot if s == 0 else jnp.where(sub >= s, pivot, pivots[t])
        factor = [None] * tiles
        for u in range(t, tiles):
            factor[u] = (jnp.where(sub > s, col[u], 0.0) if u == t else col[u]) * inverse
        for c in range(j + 1, min(j + ahead, EDGE)):
            entry = spread(cols[c][t][s : s + 1, :])
            cols[c] = [None if u < t else cols[c][u] - factor[u] * entry for u in range(tiles)]
        row = jnp.where(lane == j, 1.0, spread(rows[t][s : s + 1, :]))
        for u in range(t, tiles):
            value = jnp.where(lane == j, 0.0, rows[u]) - factor[u] * row
            rows[u] = jnp.where(sub > s, value, rows[u]) if u == t else value
        c = j + ahead
        if c < EDGE:
            cols[c] = [None if u < t else spread(rows[u][:, c : c + 1]) for u in range(tiles)]
    scale = [lax.rsqrt(p) for p in pivots]
    upper, inverse = [], []
    for u in range(tiles):
        at = sub + 8 * u
        upper.append(jnp.where(lane >= at, rows[u], 0.0) * scale[u])
        inverse.append(jnp.where(lane < at, rows[u], jnp.where(lane == at, 1.0, 0.0)) * scale[u])
    return jnp.concatenate(upper, 0), jnp.concatenate(inverse, 0)


def set_factor(gram, inverse):
    n = EDGE
    top, bottom = slice(0, n), slice(n, 2 * n)
    _, head = eliminate(gram[top, top])
    low = exact(gram[bottom, top], head, NT)
    _, tail = eliminate(gram[bottom, bottom] - exact(low, low, NT))
    inverse[top, top] = head
    inverse[top, bottom] = jnp.zeros((n, n), jnp.float32)
    inverse[bottom, bottom] = tail
    inverse[bottom, top] = -exact(tail, exact(low, head))


def set_lower(gram, lower):
    n = EDGE
    top, bottom = slice(0, n), slice(n, 2 * n)
    upper, head = eliminate(gram[top, top])
    low = exact(gram[bottom, top], head, NT)
    tail, _ = eliminate(gram[bottom, bottom] - exact(low, low, NT))
    lower[top, top] = upper.T
    lower[top, bottom] = jnp.zeros((n, n), jnp.float32)
    lower[bottom, top] = low
    lower[bottom, bottom] = tail.T


def pair_kernel(place_ref, half_ref, diag_ref, mt_ref, energy_ref, inside_ref, g, pt, tt, wt, small, li, *, scale):
    width = half_ref.shape[2]
    first, second = slice(0, width), slice(width, 2 * width)
    core = place_ref[1]
    snaps, across = 4, half_ref.shape[0] // 4
    off = len(HALVES[0]) * width // half_ref.shape[0]
    unit = half_ref.shape[1] - off
    step = math.gcd(off, width)
    for r in range(0, width, step):
        g[r : r + step, second] = half_ref[r // off, r % off : r % off + step] * scale
    g[second, first] = g[first, second].T
    for k in range(2):
        cols = slice(k * width, (k + 1) * width)
        for mine in range(2):

            @pl.when(core == mine)
            def _():
                for a in range(across):
                    to = k * width + (2 * a + mine) * unit
                    g[to : to + unit, cols] = half_ref[a * snaps + 2 * mine + k, off:] * scale
                    to = k * width + (2 * a + 1 - mine) * unit
                    g[to : to + unit, cols] = diag_ref[k, a * unit : (a + 1) * unit] * scale

    pt[...] = g[first, :] + g[second, :]
    tt[...] = exact(pt[...], g[...])
    small[...] = exact(pt[...], tt[...], NT)
    set_factor(small, li)
    wt[...] = exact(li[...], tt[...])
    pt[...] = exact(li[...], pt[...])
    energy_ref[...] = exact(wt[...], wt[...], NT)
    set_lower(energy_ref, li)
    mt_ref[...] = exact(li[...], pt[...])
    inside_ref[...] = exact(li[...], wt[...])


def vmem():
    return pl.BlockSpec(memory_space=pltpu.VMEM)


def smem():
    return pl.BlockSpec(memory_space=pltpu.SMEM)


def merge_pair(place, half, diag, scale):
    f32, width = jnp.float32, half.shape[2]
    wide = jax.ShapeDtypeStruct((width, 2 * width), f32)
    return pl.pallas_call(
        functools.partial(pair_kernel, scale=scale),
        out_shape=(wide, jax.ShapeDtypeStruct((width, width), f32), wide),
        in_specs=[smem(), vmem(), vmem()],
        out_specs=(vmem(),) * 3,
        scratch_shapes=[
            pltpu.VMEM((2 * width, 2 * width), f32),
            pltpu.VMEM((width, 2 * width), f32),
            pltpu.VMEM((width, 2 * width), f32),
            pltpu.VMEM((width, 2 * width), f32),
            pltpu.VMEM((width, width), f32),
            pltpu.VMEM((width, width), f32),
        ],
        compiler_params=pltpu.CompilerParams(vmem_limit_bytes=24 << 20),
        cost_estimate=pl.CostEstimate(flops=10**10, bytes_accessed=3 << 20, transcendentals=0),
        name="merge_pair",
    )(place, half, diag)


def cross_kernel(place_ref, mt_ref, inside_ref, mine_ref, other_ref, ahead_ref, seen_ref, x, *, scale):
    width = mt_ref.shape[0]
    snap, core = place_ref[0], place_ref[1]
    for k in range(2):
        for c in range(2):
            rows = slice(c * width, (c + 1) * width)
            rows = jnp.where(core == k, mine_ref[rows], other_ref[rows])
            x[k * width : (k + 1) * width, c * width : (c + 1) * width] = rows * scale

    @pl.when(core == 0)
    def _():
        ahead_ref[...] = exact(mt_ref[...], x[...])

    @pl.when(core == 1)
    def _():
        ahead_ref[...] = exact(mt_ref[...], x[...], NT)

    for c in range(2):
        cols = slice(c * width, (c + 1) * width)

        @pl.when(snap == 2 * core + c)
        def _():
            seen_ref[...] = inside_ref[:, cols]

        @pl.when(snap == 2 - 2 * core + c)
        def _():
            seen_ref[...] = ahead_ref[:, cols]


def look_across(place, mt, inside, mine, other, scale):
    f32, width = jnp.float32, mt.shape[0]
    return pl.pallas_call(
        functools.partial(cross_kernel, scale=scale),
        out_shape=(jax.ShapeDtypeStruct((width, 2 * width), f32), jax.ShapeDtypeStruct((width, width), f32)),
        in_specs=[smem()] + [vmem()] * 4,
        out_specs=(vmem(),) * 2,
        scratch_shapes=[pltpu.VMEM((2 * width, 2 * width), f32)],
        compiler_params=pltpu.CompilerParams(vmem_limit_bytes=24 << 20),
        name="look_across",
    )(place, mt, inside, mine, other)


def root_kernel(
    place_ref, mt_ref, energy_ref, ahead_ref, seen_ref, mt2_ref, energy2_ref, ahead2_ref, seen2_ref, own_ref,
    modes_ref, coeffs_ref, g, pt, tt, small, li, h, mhi, mlo,
):
    width = mt_ref.shape[0]
    first, second = slice(0, width), slice(width, 2 * width)
    lower_core = place_ref[1] == 0
    of_pair = lambda k, a, b: jnp.where(lower_core, (a, b)[k][...], (a, b)[1 - k][...])
    mts = [of_pair(k, mt_ref, mt2_ref) for k in range(2)]
    cross = exact(of_pair(0, ahead_ref, ahead2_ref), mts[1], NT)
    g[first, first] = of_pair(0, energy_ref, energy2_ref)
    g[first, second] = cross
    g[second, first] = cross.T
    g[second, second] = of_pair(1, energy_ref, energy2_ref)
    pt[...] = g[first, :] + g[second, :]
    tt[...] = exact(pt[...], g[...])
    small[...] = exact(pt[...], tt[...], NT)
    for k in range(2):
        mhi[k], mlo[k] = split(mts[k])
        h[k * width : (k + 1) * width] = of_pair(k, seen_ref, seen2_ref)
    set_factor(small, li)
    pt[...] = exact(li[...], pt[...])
    coeffs_ref[...] = exact(pt[...], h[...])
    khi, klo = split(pt[...])
    share = own_ref.shape[1]
    step = min(share, 256)
    for r in range(share // step):
        rows = slice(r * step, (r + 1) * step)
        total = None
        for k in range(2):
            panel = None
            for b in range(2):
                cols = slice(b * width, (b + 1) * width)
                part = own_ref[2 * k + b, rows]
                term = single(part, mhi[k, :, cols], NT) + single(part, mlo[k, :, cols], NT)
                panel = term if panel is None else panel + term
            panel = panel.astype(jnp.bfloat16)
            cols = slice(k * width, (k + 1) * width)
            term = single(panel, khi[:, cols], NT) + single(panel, klo[:, cols], NT)
            total = term if total is None else total + term
        modes_ref[rows] = total


def merge_root(place, mine, other, own):
    f32 = jnp.float32
    width = own.shape[2]
    return pl.pallas_call(
        root_kernel,
        out_shape=(jax.ShapeDtypeStruct((own.shape[1], width), f32), jax.ShapeDtypeStruct((width, width), f32)),
        in_specs=[smem()] + [vmem()] * 9,
        out_specs=(vmem(),) * 2,
        scratch_shapes=[
            pltpu.VMEM((2 * width, 2 * width), f32),
            pltpu.VMEM((width, 2 * width), f32),
            pltpu.VMEM((width, 2 * width), f32),
            pltpu.VMEM((width, width), f32),
            pltpu.VMEM((width, width), f32),
            pltpu.VMEM((2 * width, width), f32),
            pltpu.VMEM((2, width, 2 * width), jnp.bfloat16),
            pltpu.VMEM((2, width, 2 * width), jnp.bfloat16),
        ],
        compiler_params=pltpu.CompilerParams(vmem_limit_bytes=40 << 20),
        name="merge_root",
    )(place, *mine, *other, own)


def cross_gram_kernel(place_ref, own_ref, after_ref, keep_ref, send_ref):
    width = own_ref.shape[2]
    for i in range(3):
        right = jnp.concatenate([own_ref[j] for j in range(i + 1, 4)], 1)
        wide = lax.dot_general(own_ref[i], right, TN, preferred_element_type=jnp.float32)
        for j in range(i + 1, 4):
            value = wide[:, (j - i - 1) * width : (j - i) * width]
            for core in range(2):
                if (i, j) not in HALVES[core]:
                    continue
                rows = slice(HALVES[core].index((i, j)) * width, (HALVES[core].index((i, j)) + 1) * width)

                @pl.when(place_ref[1] == core)
                def _():
                    keep_ref[rows] = value

                @pl.when(place_ref[1] != core)
                def _():
                    send_ref[rows] = value


def cross_gram(place, own, after):
    width = own.shape[2]
    half = jax.ShapeDtypeStruct((len(HALVES[0]) * width, width), jnp.float32)
    return pl.pallas_call(
        cross_gram_kernel,
        out_shape=(half, half),
        in_specs=[smem(), vmem(), pl.BlockSpec(memory_space=pl.ANY)],
        out_specs=(vmem(),) * 2,
        compiler_params=pltpu.CompilerParams(vmem_limit_bytes=24 << 20),
        name="cross_gram",
    )(place, own, after)


def own_gram_kernel(snap_ref, gram_ref):
    gram_ref[...] = lax.dot_general(snap_ref[...], snap_ref[...], TN, preferred_element_type=jnp.float32)


def own_gram(snapshots):
    width = snapshots.shape[1]
    return pl.pallas_call(
        own_gram_kernel,
        out_shape=jax.ShapeDtypeStruct((width, width), jnp.float32),
        in_specs=[vmem()],
        out_specs=vmem(),
        compiler_params=pltpu.CompilerParams(vmem_limit_bytes=24 << 20),
        name="own_gram",
    )(snapshots)


def spread_sum_kernel(parts_ref, after_ref, copies_ref):
    total = parts_ref[0]
    for k in range(1, parts_ref.shape[0]):
        total = total + parts_ref[k]
    for k in range(copies_ref.shape[0]):
        copies_ref[k] = total


def spread_sum(parts, copies, after):
    return pl.pallas_call(
        spread_sum_kernel,
        out_shape=jax.ShapeDtypeStruct((copies,) + parts.shape[1:], parts.dtype),
        in_specs=[vmem(), pl.BlockSpec(memory_space=pl.ANY)],
        out_specs=vmem(),
        compiler_params=pltpu.CompilerParams(vmem_limit_bytes=8 << 20),
        name="spread_sum",
    )(parts, after)


def swap_cores(value):
    return lax.ppermute(value, "core", [(0, 1), (1, 0)])


def sum_own_gram(gram, core):
    across, planes = lax.axis_size("x"), lax.axis_size("z")
    place = lax.axis_index("x")
    piece = gram.shape[0] // across
    cut = lambda k: lax.dynamic_slice_in_dim(gram, lax.rem(place + k, across) * piece, piece, 0)
    total = cut(0)
    for part in [lax.ppermute(cut(k), "x", [(i, (i + k) % across) for i in range(across)]) for k in range(1, across)]:
        total = total + part
    total = total.reshape(2, piece // 2, -1)
    keep, send = (lax.dynamic_index_in_dim(total, c, 0, keepdims=False) for c in (core, 1 - core))
    total = keep + swap_cores(send)
    bit = 1
    while bit < planes:
        before = total
        total = total + lax.ppermute(total, "z", [(i, i ^ bit) for i in range(planes)])
        bit *= 2
    return before, total


def on_device(snapshots):
    cell_rows, width = snapshots.shape
    n_snap = lax.axis_size("y")
    share = cell_rows // n_snap
    cells = cell_rows * lax.axis_size("z") * lax.axis_size("x") * lax.axis_size("core")
    scale = 1.0 / cells
    snap, core = lax.axis_index("y"), lax.axis_index("core")
    place = jnp.stack([snap, core]).astype(jnp.int32)
    own = lax.all_to_all(snapshots.reshape(n_snap, share, width), "y", 0, 0)
    before, diag_piece = sum_own_gram(own_gram(snapshots), core)
    keep, send = cross_gram(place, own, before)
    ring = lax.axis_size(("x", "y"))
    off = keep.shape[0] // ring
    parts = lax.all_to_all((keep + swap_cores(send)).reshape(ring, off, width), ("x", "y"), 0, 0)
    piece = lax.all_to_all(spread_sum(parts, lax.axis_size("z"), diag_piece), "z", 0, 0).sum(0)
    piece = jnp.concatenate([piece, diag_piece], 0)
    half = lax.all_to_all(jnp.broadcast_to(piece, (ring,) + piece.shape), ("x", "y"), 0, 0)
    diag = half[:, off:].reshape(ring // n_snap, 2, 2, -1, width)
    diag = lax.dynamic_index_in_dim(diag, 1 - core, 1, keepdims=False).transpose(1, 0, 2, 3)
    diag = swap_cores(diag.reshape(2, width // 2, width))
    cross = half[:, :off].reshape(ring * off, width)[width:]
    mt, energy, inside = merge_pair(place, half, diag, scale)
    ahead, seen = look_across(place, mt, inside, cross, swap_cores(cross), scale)
    mine = (mt, energy, ahead, seen)
    return merge_root(place, mine, [swap_cores(value) for value in mine], own)


def solution(mesh):
    n_cell, n_snap = mesh.devices.shape
    cores, across = 2, 4
    fine = Mesh(
        mesh.devices.reshape(n_cell // (cores * across), across, cores, n_snap), ("z", "x", "core", "y")
    )
    cell = ("z", "x", "core")
    return jax.shard_map(
        on_device,
        mesh=fine,
        in_specs=(P(cell, "y"),),
        out_specs=(P(cell + ("y",), None), P(None, "y")),
        check_vma=False,
    )
```

```python
import functools
import math
import jax
import jax.numpy as jnp
from jax import lax
from jax.experimental import pallas as pl
from jax.experimental.pallas import tpu as pltpu
from jax.sharding import Mesh, PartitionSpec as P

HI = lax.Precision.HIGHEST
HALVES = (((0, 1), (0, 2), (0, 3)), ((2, 3), (1, 2), (1, 3)))
TN = (((0,), (0,)), ((), ()))
NN = (((1,), (0,)), ((), ()))
NT = (((1,), (1,)), ((), ()))
EDGE = 128


def exact(a, b, dims=NN):
    return lax.dot_general(a, b, dims, precision=HI, preferred_element_type=jnp.float32)


def split(a):
    high = a.astype(jnp.bfloat16)
    return high, (a - high.astype(jnp.float32)).astype(jnp.bfloat16)


def single(a, b, dims=NN):
    return lax.dot_general(a, b, dims, preferred_element_type=jnp.float32)


def eliminate(block, ahead=6):
    tiles = EDGE // 8
    sub = lax.broadcasted_iota(jnp.int32, (8, EDGE), 0)
    lane = lax.broadcasted_iota(jnp.int32, (8, EDGE), 1)
    spread = lambda value: jnp.broadcast_to(value, (8, EDGE))
    rows = [block[8 * u : 8 * u + 8] for u in range(tiles)]
    cols = {c: [spread(rows[u][:, c : c + 1]) for u in range(tiles)] for c in range(ahead)}
    pivots = [None] * tiles
    for j in range(EDGE):
        t, s = divmod(j, 8)
        col = cols.pop(j)
        pivot = spread(col[t][s : s + 1, :])
        inverse = 1.0 / pivot
        pivots[t] = pivot if s == 0 else jnp.where(sub >= s, pivot, pivots[t])
        factor = [None] * tiles
        for u in range(t, tiles):
            factor[u] = (jnp.where(sub > s, col[u], 0.0) if u == t else col[u]) * inverse
        for c in range(j + 1, min(j + ahead, EDGE)):
            entry = spread(cols[c][t][s : s + 1, :])
            cols[c] = [None if u < t else cols[c][u] - factor[u] * entry for u in range(tiles)]
        row = jnp.where(lane == j, 1.0, spread(rows[t][s : s + 1, :]))
        for u in range(t, tiles):
            value = jnp.where(lane == j, 0.0, rows[u]) - factor[u] * row
            rows[u] = jnp.where(sub > s, value, rows[u]) if u == t else value
        c = j + ahead
        if c < EDGE:
            cols[c] = [None if u < t else spread(rows[u][:, c : c + 1]) for u in range(tiles)]
    scale = [lax.rsqrt(p) for p in pivots]
    upper, inverse = [], []
    for u in range(tiles):
        at = sub + 8 * u
        upper.append(jnp.where(lane >= at, rows[u], 0.0) * scale[u])
        inverse.append(jnp.where(lane < at, rows[u], jnp.where(lane == at, 1.0, 0.0)) * scale[u])
    return jnp.concatenate(upper, 0), jnp.concatenate(inverse, 0)


def set_factor(gram, inverse):
    n = EDGE
    top, bottom = slice(0, n), slice(n, 2 * n)
    _, head = eliminate(gram[top, top])
    low = exact(gram[bottom, top], head, NT)
    _, tail = eliminate(gram[bottom, bottom] - exact(low, low, NT))
    inverse[top, top] = head
    inverse[top, bottom] = jnp.zeros((n, n), jnp.float32)
    inverse[bottom, bottom] = tail
    inverse[bottom, top] = -exact(tail, exact(low, head))


def set_lower(gram, lower):
    n = EDGE
    top, bottom = slice(0, n), slice(n, 2 * n)
    upper, head = eliminate(gram[top, top])
    low = exact(gram[bottom, top], head, NT)
    tail, _ = eliminate(gram[bottom, bottom] - exact(low, low, NT))
    lower[top, top] = upper.T
    lower[top, bottom] = jnp.zeros((n, n), jnp.float32)
    lower[bottom, top] = low
    lower[bottom, bottom] = tail.T


def pair_kernel(place_ref, half_ref, mt_ref, energy_ref, inside_ref, g, pt, tt, wt, small, li, *, scale):
    width = half_ref.shape[2]
    first, second = slice(0, width), slice(width, 2 * width)
    core = place_ref[1]
    snaps, across = 4, half_ref.shape[0] // 4
    off = len(HALVES[0]) * width // half_ref.shape[0]
    unit = half_ref.shape[1] - off
    step = math.gcd(off, width)
    for r in range(0, width, step):
        g[r : r + step, second] = half_ref[r // off, r % off : r % off + step] * scale
    g[second, first] = g[first, second].T
    for k in range(2):
        cols = slice(k * width, (k + 1) * width)
        for mine in range(2):

            @pl.when(core == mine)
            def _():
                for a in range(across):
                    for part, snap in ((mine, 2 * mine + k), (1 - mine, 2 - 2 * mine + k)):
                        to = k * width + (2 * a + part) * unit
                        g[to : to + unit, cols] = half_ref[a * snaps + snap, off:] * scale

    pt[...] = g[first, :] + g[second, :]
    tt[...] = exact(pt[...], g[...])
    small[...] = exact(pt[...], tt[...], NT)
    set_factor(small, li)
    wt[...] = exact(li[...], tt[...])
    pt[...] = exact(li[...], pt[...])
    energy_ref[...] = exact(wt[...], wt[...], NT)
    set_lower(energy_ref, li)
    mt_ref[...] = exact(li[...], pt[...])
    inside_ref[...] = exact(li[...], wt[...])


def vmem():
    return pl.BlockSpec(memory_space=pltpu.VMEM)


def smem():
    return pl.BlockSpec(memory_space=pltpu.SMEM)


def merge_pair(place, half, scale):
    f32, width = jnp.float32, half.shape[2]
    wide = jax.ShapeDtypeStruct((width, 2 * width), f32)
    return pl.pallas_call(
        functools.partial(pair_kernel, scale=scale),
        out_shape=(wide, jax.ShapeDtypeStruct((width, width), f32), wide),
        in_specs=[smem(), vmem()],
        out_specs=(vmem(),) * 3,
        scratch_shapes=[
            pltpu.VMEM((2 * width, 2 * width), f32),
            pltpu.VMEM((width, 2 * width), f32),
            pltpu.VMEM((width, 2 * width), f32),
            pltpu.VMEM((width, 2 * width), f32),
            pltpu.VMEM((width, width), f32),
            pltpu.VMEM((width, width), f32),
        ],
        compiler_params=pltpu.CompilerParams(vmem_limit_bytes=24 << 20),
        cost_estimate=pl.CostEstimate(flops=10**10, bytes_accessed=3 << 20, transcendentals=0),
        name="merge_pair",
    )(place, half)


def cross_kernel(place_ref, mt_ref, inside_ref, mine_ref, other_ref, ahead_ref, seen_ref, x, *, scale):
    width = mt_ref.shape[0]
    snap, core = place_ref[0], place_ref[1]
    for k in range(2):
        for c in range(2):
            rows = slice(c * width, (c + 1) * width)
            rows = jnp.where(core == k, mine_ref[rows], other_ref[rows])
            x[k * width : (k + 1) * width, c * width : (c + 1) * width] = rows * scale

    @pl.when(core == 0)
    def _():
        ahead_ref[...] = exact(mt_ref[...], x[...])

    @pl.when(core == 1)
    def _():
        ahead_ref[...] = exact(mt_ref[...], x[...], NT)

    for c in range(2):
        cols = slice(c * width, (c + 1) * width)

        @pl.when(snap == 2 * core + c)
        def _():
            seen_ref[...] = inside_ref[:, cols]

        @pl.when(snap == 2 - 2 * core + c)
        def _():
            seen_ref[...] = ahead_ref[:, cols]


def look_across(place, mt, inside, mine, other, scale):
    f32, width = jnp.float32, mt.shape[0]
    return pl.pallas_call(
        functools.partial(cross_kernel, scale=scale),
        out_shape=(jax.ShapeDtypeStruct((width, 2 * width), f32), jax.ShapeDtypeStruct((width, width), f32)),
        in_specs=[smem()] + [vmem()] * 4,
        out_specs=(vmem(),) * 2,
        scratch_shapes=[pltpu.VMEM((2 * width, 2 * width), f32)],
        compiler_params=pltpu.CompilerParams(vmem_limit_bytes=24 << 20),
        name="look_across",
    )(place, mt, inside, mine, other)


def root_kernel(
    place_ref, mt_ref, energy_ref, ahead_ref, seen_ref, mt2_ref, energy2_ref, ahead2_ref, seen2_ref, own_ref,
    modes_ref, coeffs_ref, g, pt, tt, small, li, h, mhi, mlo,
):
    width = mt_ref.shape[0]
    first, second = slice(0, width), slice(width, 2 * width)
    lower_core = place_ref[1] == 0
    of_pair = lambda k, a, b: jnp.where(lower_core, (a, b)[k][...], (a, b)[1 - k][...])
    mts = [of_pair(k, mt_ref, mt2_ref) for k in range(2)]
    cross = exact(of_pair(0, ahead_ref, ahead2_ref), mts[1], NT)
    g[first, first] = of_pair(0, energy_ref, energy2_ref)
    g[first, second] = cross
    g[second, first] = cross.T
    g[second, second] = of_pair(1, energy_ref, energy2_ref)
    pt[...] = g[first, :] + g[second, :]
    tt[...] = exact(pt[...], g[...])
    small[...] = exact(pt[...], tt[...], NT)
    for k in range(2):
        mhi[k], mlo[k] = split(mts[k])
        h[k * width : (k + 1) * width] = of_pair(k, seen_ref, seen2_ref)
    set_factor(small, li)
    pt[...] = exact(li[...], pt[...])
    coeffs_ref[...] = exact(pt[...], h[...])
    khi, klo = split(pt[...])
    total = None
    for k in range(2):
        panel = None
        for b in range(2):
            cols = slice(b * width, (b + 1) * width)
            part = own_ref[2 * k + b]
            term = single(part, mhi[k, :, cols], NT) + single(part, mlo[k, :, cols], NT)
            panel = term if panel is None else panel + term
        panel = panel.astype(jnp.bfloat16)
        cols = slice(k * width, (k + 1) * width)
        term = single(panel, khi[:, cols], NT) + single(panel, klo[:, cols], NT)
        total = term if total is None else total + term
    modes_ref[...] = total


def merge_root(place, mine, other, own):
    f32 = jnp.float32
    width = own.shape[2]
    return pl.pallas_call(
        root_kernel,
        out_shape=(jax.ShapeDtypeStruct((own.shape[1], width), f32), jax.ShapeDtypeStruct((width, width), f32)),
        in_specs=[smem()] + [vmem()] * 9,
        out_specs=(vmem(),) * 2,
        scratch_shapes=[
            pltpu.VMEM((2 * width, 2 * width), f32),
            pltpu.VMEM((width, 2 * width), f32),
            pltpu.VMEM((width, 2 * width), f32),
            pltpu.VMEM((width, width), f32),
            pltpu.VMEM((width, width), f32),
            pltpu.VMEM((2 * width, width), f32),
            pltpu.VMEM((2, width, 2 * width), jnp.bfloat16),
            pltpu.VMEM((2, width, 2 * width), jnp.bfloat16),
        ],
        compiler_params=pltpu.CompilerParams(vmem_limit_bytes=40 << 20),
        name="merge_root",
    )(place, *mine, *other, own)


def cross_gram_kernel(place_ref, own_ref, after_ref, keep_ref, send_ref):
    width = own_ref.shape[2]
    for i in range(3):
        right = jnp.concatenate([own_ref[j] for j in range(i + 1, 4)], 1)
        wide = lax.dot_general(own_ref[i], right, TN, preferred_element_type=jnp.float32)
        for j in range(i + 1, 4):
            value = wide[:, (j - i - 1) * width : (j - i) * width]
            for core in range(2):
                if (i, j) not in HALVES[core]:
                    continue
                rows = slice(HALVES[core].index((i, j)) * width, (HALVES[core].index((i, j)) + 1) * width)

                @pl.when(place_ref[1] == core)
                def _():
                    keep_ref[rows] = value

                @pl.when(place_ref[1] != core)
                def _():
                    send_ref[rows] = value


def cross_gram(place, own, after):
    width = own.shape[2]
    half = jax.ShapeDtypeStruct((len(HALVES[0]) * width, width), jnp.float32)
    return pl.pallas_call(
        cross_gram_kernel,
        out_shape=(half, half),
        in_specs=[smem(), vmem(), pl.BlockSpec(memory_space=pl.ANY)],
        out_specs=(vmem(),) * 2,
        compiler_params=pltpu.CompilerParams(vmem_limit_bytes=24 << 20),
        name="cross_gram",
    )(place, own, after)


def own_gram_kernel(snap_ref, gram_ref):
    gram_ref[...] = lax.dot_general(snap_ref[...], snap_ref[...], TN, preferred_element_type=jnp.float32)


def own_gram(snapshots):
    width = snapshots.shape[1]
    return pl.pallas_call(
        own_gram_kernel,
        out_shape=jax.ShapeDtypeStruct((width, width), jnp.float32),
        in_specs=[vmem()],
        out_specs=vmem(),
        compiler_params=pltpu.CompilerParams(vmem_limit_bytes=24 << 20),
        name="own_gram",
    )(snapshots)


def spread_sum_kernel(parts_ref, after_ref, copies_ref):
    total = parts_ref[0]
    for k in range(1, parts_ref.shape[0]):
        total = total + parts_ref[k]
    for k in range(copies_ref.shape[0]):
        copies_ref[k] = total


def spread_sum(parts, copies, after):
    return pl.pallas_call(
        spread_sum_kernel,
        out_shape=jax.ShapeDtypeStruct((copies,) + parts.shape[1:], parts.dtype),
        in_specs=[vmem(), pl.BlockSpec(memory_space=pl.ANY)],
        out_specs=vmem(),
        compiler_params=pltpu.CompilerParams(vmem_limit_bytes=8 << 20),
        name="spread_sum",
    )(parts, after)


def swap_cores(value):
    return lax.ppermute(value, "core", [(0, 1), (1, 0)])


def sum_own_gram(gram, core):
    across, planes = lax.axis_size("x"), lax.axis_size("z")
    place = lax.axis_index("x")
    piece = gram.shape[0] // across
    cut = lambda k: lax.dynamic_slice_in_dim(gram, lax.rem(place + k, across) * piece, piece, 0)
    total = cut(0)
    for part in [lax.ppermute(cut(k), "x", [(i, (i + k) % across) for i in range(across)]) for k in range(1, across)]:
        total = total + part
    total = total.reshape(2, piece // 2, -1)
    keep, send = (lax.dynamic_index_in_dim(total, c, 0, keepdims=False) for c in (core, 1 - core))
    total = keep + swap_cores(send)
    bit = 1
    while bit < planes:
        before = total
        total = total + lax.ppermute(total, "z", [(i, i ^ bit) for i in range(planes)])
        bit *= 2
    return before, total


def fit_pair(piece, snap, core):
    n_snap = lax.axis_size("y")
    half = n_snap // 2
    trades = [
        (c * n_snap + y, (1 - c) * n_snap + (y + half) % n_snap)
        for c in range(2)
        for y in range(n_snap)
        if y // half != c
    ]
    return jnp.where(snap // half == core, piece, lax.ppermute(piece, ("core", "y"), trades))


def on_device(snapshots):
    cell_rows, width = snapshots.shape
    n_snap = lax.axis_size("y")
    share = cell_rows // n_snap
    cells = cell_rows * lax.axis_size("z") * lax.axis_size("x") * lax.axis_size("core")
    scale = 1.0 / cells
    snap, core = lax.axis_index("y"), lax.axis_index("core")
    place = jnp.stack([snap, core]).astype(jnp.int32)
    own = lax.all_to_all(snapshots.reshape(n_snap, share, width), "y", 0, 0)
    before, diag_piece = sum_own_gram(own_gram(snapshots), core)
    diag_piece = fit_pair(diag_piece, snap, core)
    keep, send = cross_gram(place, own, before)
    ring = lax.axis_size(("x", "y"))
    off = keep.shape[0] // ring
    parts = lax.all_to_all((keep + swap_cores(send)).reshape(ring, off, width), ("x", "y"), 0, 0)
    piece = lax.all_to_all(spread_sum(parts, lax.axis_size("z"), diag_piece), "z", 0, 0).sum(0)
    piece = jnp.concatenate([piece, diag_piece], 0)
    half = lax.all_to_all(jnp.broadcast_to(piece, (ring,) + piece.shape), ("x", "y"), 0, 0)
    cross = half[:, :off].reshape(ring * off, width)[width:]
    mt, energy, inside = merge_pair(place, half, scale)
    ahead, seen = look_across(place, mt, inside, cross, swap_cores(cross), scale)
    mine = (mt, energy, ahead, seen)
    return merge_root(place, mine, [swap_cores(value) for value in mine], own)


def solution(mesh):
    n_cell, n_snap = mesh.devices.shape
    cores, across = 2, 4
    fine = Mesh(
        mesh.devices.reshape(n_cell // (cores * across), across, cores, n_snap), ("z", "x", "core", "y")
    )
    cell = ("z", "x", "core")
    return jax.shard_map(
        on_device,
        mesh=fine,
        in_specs=(P(cell, "y"),),
        out_specs=(P(cell + ("y",), None), P(None, "y")),
        check_vma=False,
    )
```

```python
import functools
import math
import jax
import jax.numpy as jnp
from jax import lax
from jax.experimental import pallas as pl
from jax.experimental.pallas import tpu as pltpu
from jax.sharding import Mesh, PartitionSpec as P

HI = lax.Precision.HIGHEST
HALVES = (((0, 1), (0, 2), (0, 3)), ((2, 3), (1, 2), (1, 3)))
TN = (((0,), (0,)), ((), ()))
NN = (((1,), (0,)), ((), ()))
NT = (((1,), (1,)), ((), ()))
EDGE = 128


def exact(a, b, dims=NN):
    return lax.dot_general(a, b, dims, precision=HI, preferred_element_type=jnp.float32)


def split(a):
    high = a.astype(jnp.bfloat16)
    return high, (a - high.astype(jnp.float32)).astype(jnp.bfloat16)


def single(a, b, dims=NN):
    return lax.dot_general(a, b, dims, preferred_element_type=jnp.float32)


def eliminate(block, ahead=6):
    tiles = EDGE // 8
    sub = lax.broadcasted_iota(jnp.int32, (8, EDGE), 0)
    lane = lax.broadcasted_iota(jnp.int32, (8, EDGE), 1)
    spread = lambda value: jnp.broadcast_to(value, (8, EDGE))
    rows = [block[8 * u : 8 * u + 8] for u in range(tiles)]
    cols = {c: [spread(rows[u][:, c : c + 1]) for u in range(tiles)] for c in range(ahead)}
    pivots = [None] * tiles
    for j in range(EDGE):
        t, s = divmod(j, 8)
        col = cols.pop(j)
        pivot = spread(col[t][s : s + 1, :])
        inverse = 1.0 / pivot
        pivots[t] = pivot if s == 0 else jnp.where(sub >= s, pivot, pivots[t])
        factor = [None] * tiles
        for u in range(t, tiles):
            factor[u] = (jnp.where(sub > s, col[u], 0.0) if u == t else col[u]) * inverse
        for c in range(j + 1, min(j + ahead, EDGE)):
            entry = spread(cols[c][t][s : s + 1, :])
            cols[c] = [None if u < t else cols[c][u] - factor[u] * entry for u in range(tiles)]
        row = jnp.where(lane == j, 1.0, spread(rows[t][s : s + 1, :]))
        for u in range(t, tiles):
            value = jnp.where(lane == j, 0.0, rows[u]) - factor[u] * row
            rows[u] = jnp.where(sub > s, value, rows[u]) if u == t else value
        c = j + ahead
        if c < EDGE:
            cols[c] = [None if u < t else spread(rows[u][:, c : c + 1]) for u in range(tiles)]
    scale = [lax.rsqrt(p) for p in pivots]
    upper, inverse = [], []
    for u in range(tiles):
        at = sub + 8 * u
        upper.append(jnp.where(lane >= at, rows[u], 0.0) * scale[u])
        inverse.append(jnp.where(lane < at, rows[u], jnp.where(lane == at, 1.0, 0.0)) * scale[u])
    return jnp.concatenate(upper, 0), jnp.concatenate(inverse, 0)


def set_factor(gram, inverse):
    n = EDGE
    top, bottom = slice(0, n), slice(n, 2 * n)
    _, head = eliminate(gram[top, top])
    low = exact(gram[bottom, top], head, NT)
    _, tail = eliminate(gram[bottom, bottom] - exact(low, low, NT))
    inverse[top, top] = head
    inverse[top, bottom] = jnp.zeros((n, n), jnp.float32)
    inverse[bottom, bottom] = tail
    inverse[bottom, top] = -exact(tail, exact(low, head))


def set_lower(gram, lower):
    n = EDGE
    top, bottom = slice(0, n), slice(n, 2 * n)
    upper, head = eliminate(gram[top, top])
    low = exact(gram[bottom, top], head, NT)
    tail, _ = eliminate(gram[bottom, bottom] - exact(low, low, NT))
    lower[top, top] = upper.T
    lower[top, bottom] = jnp.zeros((n, n), jnp.float32)
    lower[bottom, top] = low
    lower[bottom, bottom] = tail.T


def pair_kernel(place_ref, half_ref, diag_ref, mt_ref, energy_ref, inside_ref, g, pt, tt, wt, small, li, *, scale):
    width = half_ref.shape[2]
    first, second = slice(0, width), slice(width, 2 * width)
    core = place_ref[1]
    snaps, across = 4, half_ref.shape[0] // 4
    off = len(HALVES[0]) * width // half_ref.shape[0]
    unit = half_ref.shape[1] - off
    step = math.gcd(off, width)
    for r in range(0, width, step):
        g[r : r + step, second] = half_ref[r // off, r % off : r % off + step] * scale
    g[second, first] = g[first, second].T
    for k in range(2):
        cols = slice(k * width, (k + 1) * width)
        for mine in range(2):

            @pl.when(core == mine)
            def _():
                for a in range(across):
                    to = k * width + (2 * a + mine) * unit
                    g[to : to + unit, cols] = half_ref[a * snaps + 2 * mine + k, off:] * scale
                    to = k * width + (2 * a + 1 - mine) * unit
                    g[to : to + unit, cols] = diag_ref[k, a * unit : (a + 1) * unit] * scale

    pt[...] = g[first, :] + g[second, :]
    tt[...] = exact(pt[...], g[...])
    small[...] = exact(pt[...], tt[...], NT)
    set_factor(small, li)
    wt[...] = exact(li[...], tt[...])
    pt[...] = exact(li[...], pt[...])
    energy_ref[...] = exact(wt[...], wt[...], NT)
    set_lower(energy_ref, li)
    mt_ref[...] = exact(li[...], pt[...])
    inside_ref[...] = exact(li[...], wt[...])


def vmem():
    return pl.BlockSpec(memory_space=pltpu.VMEM)


def smem():
    return pl.BlockSpec(memory_space=pltpu.SMEM)


def merge_pair(place, half, diag, scale):
    f32, width = jnp.float32, half.shape[2]
    wide = jax.ShapeDtypeStruct((width, 2 * width), f32)
    return pl.pallas_call(
        functools.partial(pair_kernel, scale=scale),
        out_shape=(wide, jax.ShapeDtypeStruct((width, width), f32), wide),
        in_specs=[smem(), vmem(), vmem()],
        out_specs=(vmem(),) * 3,
        scratch_shapes=[
            pltpu.VMEM((2 * width, 2 * width), f32),
            pltpu.VMEM((width, 2 * width), f32),
            pltpu.VMEM((width, 2 * width), f32),
            pltpu.VMEM((width, 2 * width), f32),
            pltpu.VMEM((width, width), f32),
            pltpu.VMEM((width, width), f32),
        ],
        compiler_params=pltpu.CompilerParams(vmem_limit_bytes=24 << 20),
        cost_estimate=pl.CostEstimate(flops=10**10, bytes_accessed=3 << 20, transcendentals=0),
        name="merge_pair",
    )(place, half, diag)


def cross_kernel(place_ref, mt_ref, inside_ref, mine_ref, other_ref, ahead_ref, seen_ref, x, *, scale):
    width = mt_ref.shape[0]
    snap, core = place_ref[0], place_ref[1]
    for k in range(2):
        for c in range(2):
            rows = slice(c * width, (c + 1) * width)
            rows = jnp.where(core == k, mine_ref[rows], other_ref[rows])
            x[k * width : (k + 1) * width, c * width : (c + 1) * width] = rows * scale

    @pl.when(core == 0)
    def _():
        ahead_ref[...] = exact(mt_ref[...], x[...])

    @pl.when(core == 1)
    def _():
        ahead_ref[...] = exact(mt_ref[...], x[...], NT)

    for c in range(2):
        cols = slice(c * width, (c + 1) * width)

        @pl.when(snap == 2 * core + c)
        def _():
            seen_ref[...] = inside_ref[:, cols]

        @pl.when(snap == 2 - 2 * core + c)
        def _():
            seen_ref[...] = ahead_ref[:, cols]


def look_across(place, mt, inside, mine, other, scale):
    f32, width = jnp.float32, mt.shape[0]
    return pl.pallas_call(
        functools.partial(cross_kernel, scale=scale),
        out_shape=(jax.ShapeDtypeStruct((width, 2 * width), f32), jax.ShapeDtypeStruct((width, width), f32)),
        in_specs=[smem()] + [vmem()] * 4,
        out_specs=(vmem(),) * 2,
        scratch_shapes=[pltpu.VMEM((2 * width, 2 * width), f32)],
        compiler_params=pltpu.CompilerParams(vmem_limit_bytes=24 << 20),
        name="look_across",
    )(place, mt, inside, mine, other)


def root_kernel(
    place_ref, mt_ref, energy_ref, ahead_ref, seen_ref, mt2_ref, energy2_ref, ahead2_ref, seen2_ref, own_ref,
    modes_ref, coeffs_ref, g, pt, tt, small, li, h, mhi, mlo,
):
    width = mt_ref.shape[0]
    first, second = slice(0, width), slice(width, 2 * width)
    lower_core = place_ref[1] == 0
    of_pair = lambda k, a, b: jnp.where(lower_core, (a, b)[k][...], (a, b)[1 - k][...])
    mts = [of_pair(k, mt_ref, mt2_ref) for k in range(2)]
    cross = exact(of_pair(0, ahead_ref, ahead2_ref), mts[1], NT)
    g[first, first] = of_pair(0, energy_ref, energy2_ref)
    g[first, second] = cross
    g[second, first] = cross.T
    g[second, second] = of_pair(1, energy_ref, energy2_ref)
    pt[...] = g[first, :] + g[second, :]
    tt[...] = exact(pt[...], g[...])
    small[...] = exact(pt[...], tt[...], NT)
    for k in range(2):
        mhi[k], mlo[k] = split(mts[k])
        h[k * width : (k + 1) * width] = of_pair(k, seen_ref, seen2_ref)
    set_factor(small, li)
    pt[...] = exact(li[...], pt[...])
    coeffs_ref[...] = exact(pt[...], h[...])
    khi, klo = split(pt[...])
    total = None
    for k in range(2):
        panel = None
        for b in range(2):
            cols = slice(b * width, (b + 1) * width)
            part = own_ref[2 * k + b]
            term = single(part, mhi[k, :, cols], NT) + single(part, mlo[k, :, cols], NT)
            panel = term if panel is None else panel + term
        panel = panel.astype(jnp.bfloat16)
        cols = slice(k * width, (k + 1) * width)
        term = single(panel, khi[:, cols], NT) + single(panel, klo[:, cols], NT)
        total = term if total is None else total + term
    modes_ref[...] = total


def merge_root(place, mine, other, own):
    f32 = jnp.float32
    width = own.shape[2]
    return pl.pallas_call(
        root_kernel,
        out_shape=(jax.ShapeDtypeStruct((own.shape[1], width), f32), jax.ShapeDtypeStruct((width, width), f32)),
        in_specs=[smem()] + [vmem()] * 9,
        out_specs=(vmem(),) * 2,
        scratch_shapes=[
            pltpu.VMEM((2 * width, 2 * width), f32),
            pltpu.VMEM((width, 2 * width), f32),
            pltpu.VMEM((width, 2 * width), f32),
            pltpu.VMEM((width, width), f32),
            pltpu.VMEM((width, width), f32),
            pltpu.VMEM((2 * width, width), f32),
            pltpu.VMEM((2, width, 2 * width), jnp.bfloat16),
            pltpu.VMEM((2, width, 2 * width), jnp.bfloat16),
        ],
        compiler_params=pltpu.CompilerParams(vmem_limit_bytes=40 << 20),
        name="merge_root",
    )(place, *mine, *other, own)


def cross_gram_kernel(place_ref, own_ref, after_ref, keep_ref, send_ref):
    width = own_ref.shape[2]
    for i in range(3):
        right = jnp.concatenate([own_ref[j] for j in range(i + 1, 4)], 1)
        wide = lax.dot_general(own_ref[i], right, TN, preferred_element_type=jnp.float32)
        for j in range(i + 1, 4):
            value = wide[:, (j - i - 1) * width : (j - i) * width]
            for core in range(2):
                if (i, j) not in HALVES[core]:
                    continue
                rows = slice(HALVES[core].index((i, j)) * width, (HALVES[core].index((i, j)) + 1) * width)

                @pl.when(place_ref[1] == core)
                def _():
                    keep_ref[rows] = value

                @pl.when(place_ref[1] != core)
                def _():
                    send_ref[rows] = value


def cross_gram(place, own, after):
    width = own.shape[2]
    half = jax.ShapeDtypeStruct((len(HALVES[0]) * width, width), jnp.float32)
    return pl.pallas_call(
        cross_gram_kernel,
        out_shape=(half, half),
        in_specs=[smem(), vmem(), pl.BlockSpec(memory_space=pl.ANY)],
        out_specs=(vmem(),) * 2,
        compiler_params=pltpu.CompilerParams(vmem_limit_bytes=24 << 20),
        name="cross_gram",
    )(place, own, after)


def own_gram_kernel(snap_ref, gram_ref):
    gram_ref[...] = lax.dot_general(snap_ref[...], snap_ref[...], TN, preferred_element_type=jnp.float32)


def own_gram(snapshots):
    width = snapshots.shape[1]
    return pl.pallas_call(
        own_gram_kernel,
        out_shape=jax.ShapeDtypeStruct((width, width), jnp.float32),
        in_specs=[vmem()],
        out_specs=vmem(),
        compiler_params=pltpu.CompilerParams(vmem_limit_bytes=24 << 20),
        name="own_gram",
    )(snapshots)


def spread_sum_kernel(parts_ref, after_ref, copies_ref):
    total = parts_ref[0]
    for k in range(1, parts_ref.shape[0]):
        total = total + parts_ref[k]
    for k in range(copies_ref.shape[0]):
        copies_ref[k] = total


def spread_sum(parts, copies, after):
    return pl.pallas_call(
        spread_sum_kernel,
        out_shape=jax.ShapeDtypeStruct((copies,) + parts.shape[1:], parts.dtype),
        in_specs=[vmem(), pl.BlockSpec(memory_space=pl.ANY)],
        out_specs=vmem(),
        compiler_params=pltpu.CompilerParams(vmem_limit_bytes=8 << 20),
        name="spread_sum",
    )(parts, after)


def swap_cores(value):
    return lax.ppermute(value, "core", [(0, 1), (1, 0)])


def sum_own_gram(gram, core):
    across, planes = lax.axis_size("x"), lax.axis_size("z")
    place = lax.axis_index("x")
    piece = gram.shape[0] // across
    cut = lambda k: lax.dynamic_slice_in_dim(gram, lax.rem(place + k, across) * piece, piece, 0)
    total = cut(0)
    for part in [lax.ppermute(cut(k), "x", [(i, (i + k) % across) for i in range(across)]) for k in range(1, across)]:
        total = total + part
    total = total.reshape(2, piece // 2, -1)
    keep, send = (lax.dynamic_index_in_dim(total, c, 0, keepdims=False) for c in (core, 1 - core))
    total = keep + swap_cores(send)
    bit = 1
    while bit < planes:
        before = total
        total = total + lax.ppermute(total, "z", [(i, i ^ bit) for i in range(planes)])
        bit *= 2
    return before, total


def on_device(snapshots):
    cell_rows, width = snapshots.shape
    n_snap = lax.axis_size("y")
    share = cell_rows // n_snap
    cells = cell_rows * lax.axis_size("z") * lax.axis_size("x") * lax.axis_size("core")
    scale = 1.0 / cells
    snap, core = lax.axis_index("y"), lax.axis_index("core")
    place = jnp.stack([snap, core]).astype(jnp.int32)
    own = lax.all_to_all(snapshots.reshape(n_snap, share, width), "y", 0, 0)
    before, diag_piece = sum_own_gram(own_gram(snapshots), core)
    keep, send = cross_gram(place, own, before)
    ring = lax.axis_size(("x", "y"))
    off = keep.shape[0] // ring
    parts = lax.all_to_all((keep + swap_cores(send)).reshape(ring, off, width), ("x", "y"), 0, 0)
    piece = lax.all_to_all(spread_sum(parts, lax.axis_size("z"), diag_piece), "z", 0, 0).sum(0)
    piece = jnp.concatenate([piece, diag_piece], 0)
    half = lax.all_to_all(jnp.broadcast_to(piece, (ring,) + piece.shape), ("x", "y"), 0, 0)
    diag = half[:, off:].reshape(ring // n_snap, 2, 2, -1, width)
    diag = lax.dynamic_index_in_dim(diag, 1 - core, 1, keepdims=False).transpose(1, 0, 2, 3)
    diag = swap_cores(diag.reshape(2, width // 2, width))
    cross = half[:, :off].reshape(ring * off, width)[width:]
    mt, energy, inside = merge_pair(place, half, diag, scale)
    ahead, seen = look_across(place, mt, inside, cross, swap_cores(cross), scale)
    mine = (mt, energy, ahead, seen)
    return merge_root(place, mine, [swap_cores(value) for value in mine], own)


def solution(mesh):
    n_cell, n_snap = mesh.devices.shape
    cores, across = 2, 4
    fine = Mesh(
        mesh.devices.reshape(n_cell // (cores * across), across, cores, n_snap), ("z", "x", "core", "y")
    )
    cell = ("z", "x", "core")
    return jax.shard_map(
        on_device,
        mesh=fine,
        in_specs=(P(cell, "y"),),
        out_specs=(P(cell + ("y",), None), P(None, "y")),
        check_vma=False,
    )
```
